512 devices in a mesh: region: 16 (over z, core), dev: 32 (over y, x).
Axes of the slice: x: 4, y: 8, z: 8, core: 2. Of those that a mesh axis runs over, the one named last changes fastest.
Arguments:
- basis_values: bfloat16 [6144, 4, 256, 128], P(('region', 'dev')), may hold values from -6 to 6
- density_rows: bfloat16 [1536, 4, 128, 128], P(('region', 'dev')), may hold values from -0.013671875 to 0.013671875
- block_mask: int32 [1536, 4], P(('region', 'dev')), may hold values 0 or 1
- window_start: int32 [512], P(('region', 'dev')), may hold values from 0 to 95
- batch_offsets: int32 [512, 12], P(('region', 'dev')), may hold values from 0 to 28, as said below
- batch_sizes: int32 [512, 12], P(('region', 'dev')), may hold values from 1 to 256, 1920 in all within a row
- atom_near: int32 [6144, 6], P(('region', 'dev')), may hold values from 0 to 1535
- harmonics: bfloat16 [6144, 6, 25, 256], P(('region', 'dev')), may hold values from -6 to 6
- partition: float32 [6144, 6, 256], P(('region', 'dev')), may hold values from 0.002 to 0.05
- radius: float32 [6144, 6, 256], P(('region', 'dev')), may hold values from 0 to 15
- radial_table: float32 [25, 16], replicated, may hold values from -1.5 to 1.5
Outputs:
- density: float32 [6144, 256], P(('region', 'dev'))
- moments: float32 [25, 8192], P(None, ('region', 'dev'))
- potential: float32 [6144, 256], P(('region', 'dev'))
The draws below stay inside these ranges and needn't reach their ends.
Inputs may be any that keep to these rules, and one draw needn't show every extreme that they name: The blocks of a batch are positions batch_offsets to batch_offsets + 3 of its device's window of 32 consecutive blocks.
All inputs are finite; a program needn't handle non-finite values. No bound on the sum of `block_mask` on one device may be relied on, other than what follows from the above.
Results may differ from the reference program's by a relative error of at most 0.0029.
Values may be sent and summed in bfloat16 or wider, within the bound.
A program may use at most 64 MiB of HBM per device.

```python
import math
import jax
import jax.numpy as jnp
import numpy as np
from jax import lax

BS = 128
PTS = 256
NNB = 4
KB = 4
BLK_DEV = 3
LM = 25
NR = 16
NAT = 6
ATOM_DEV = 16
BATCH_DEV = 12
WIN = 32
NB = 96
ATOMS = 8192
NBT = 6144
TOTAL_DEV = 1920
N_REGION = 16
N_DEV = 32


def draw_batch_offsets(key, part):
    row_total = N_REGION * N_DEV
    top_value = WIN - NNB
    drawn = jax.random.randint(jax.random.fold_in(key, 11), (row_total, BATCH_DEV), 0, top_value + 1)
    low_position = jax.random.randint(jax.random.fold_in(key, 12), (row_total, 1), 0, BATCH_DEV)
    step_value = jax.random.randint(jax.random.fold_in(key, 13), (row_total, 1), 1, BATCH_DEV)
    high_position = (low_position + step_value) % BATCH_DEV
    column = jnp.arange(BATCH_DEV)[None, :]
    drawn = jnp.where(column == low_position, 0, drawn)
    drawn = jnp.where(column == high_position, top_value, drawn)
    return drawn.astype(jnp.int32)


def set_ends(result, rng, least, high):
    longest = result.shape.index(max(result.shape))
    spots = []
    for shift in (0, 1):
        where = [jax.random.randint(jax.random.fold_in(rng, axis), (), 0, length) for axis, length in enumerate(result.shape)]
        where[longest] = (where[longest] + shift) % result.shape[longest]
        spots.append(tuple(where))
    return result.at[spots[0]].set(least).at[spots[1]].set(high)


def block_levels(rng, extent, pieces, least, high):
    factor_of = 1.0
    for position, blocks in pieces:
        draws = jax.random.uniform(jax.random.fold_in(jax.random.fold_in(rng, 6), position), (blocks,), jnp.float32, least / len(pieces), high / len(pieces))
        factor_of = factor_of * jnp.repeat(jnp.exp(draws), extent[position] // blocks).reshape((-1,) + (1,) * (len(extent) - 1 - position))
    return factor_of


def split_up(count, total, most, slope):
    weights = [(1 << 20) // math.isqrt(rank ** slope) + 1 for rank in range(2, count + 1)]
    rest, counts = total - most - (count - 1), [1] * (count - 1)
    while rest > 0:
        movable = [i for i in range(count - 1) if counts[i] < most]
        mass, left = sum([weights[i] for i in movable]), rest
        for i in movable:
            extra = min(most - counts[i], max(1, left * weights[i] // mass), rest)
            counts[i] = counts[i] + extra
            rest = rest - extra
    return np.array([most] + counts)


def ragged_sizes(stream_key, amount, total, bound, slope):
    if amount == 2:
        one = jax.random.randint(stream_key, (), max(1, total - bound), min(bound, total - 1) + 1)
        return jnp.stack([one, total - one])
    lengths = jnp.asarray(split_up(amount, total, bound, slope), jnp.int32)
    twos = (amount - 1) // 2
    source_of, receiver = lengths[1:1 + 2 * twos:2], lengths[2:2 + 2 * twos:2]
    margin = jnp.minimum(source_of - 1, bound - receiver)
    moved = jax.random.randint(jax.random.fold_in(stream_key, 1), (twos,), 0, 1 << 20) % (margin + 1)
    lengths = lengths.at[1:1 + 2 * twos:2].set(source_of - moved).at[2:2 + 2 * twos:2].set(receiver + moved)
    return lengths[jax.random.permutation(jax.random.fold_in(stream_key, 2), amount)]


def scatter_about(key, dims, scale, reach, cuts=(), held_as=jnp.bfloat16):
    level = block_levels(key, dims, cuts, -0.22, 0.18) if cuts else 1.0
    values = jax.random.normal(key, dims, jnp.float32) * scale * level
    return jnp.minimum(jnp.maximum(values, -reach), reach).astype(held_as)


def setup_inputs(seed: int = 0) -> dict:
    key_of = jax.random.split(jax.random.key(seed), 12)
    return {
        "basis_values": scatter_about(key_of[0], (NBT, NNB, PTS, BS), 1.0, 6.0, ((0, 512),)),
        "density_rows": scatter_about(key_of[1], (N_REGION * NB, KB, BS, BS), (12 * BS * BS) ** -0.5, 0.013671875, ((0, 512),)),
        "block_mask": set_ends((jax.random.randint(key_of[2], (N_REGION * NB, KB), 0, 4) < 3).astype(jnp.int32), jax.random.fold_in(key_of[2], 1), 0, 1),
        "window_start": set_ends(jax.random.randint(key_of[3], (N_REGION * N_DEV,), 0, BLK_DEV * N_DEV), jax.random.fold_in(key_of[3], 1), 0, (BLK_DEV * N_DEV) - 1).astype(jnp.int32),
        "batch_offsets": draw_batch_offsets(jax.random.fold_in(key_of[11], 71), 0),
        "batch_sizes": jax.vmap(lambda own: ragged_sizes(own, BATCH_DEV, TOTAL_DEV, PTS, 2))(jax.random.split(key_of[5], (N_REGION * N_DEV))).reshape((N_REGION * N_DEV, BATCH_DEV)).astype(jnp.int32),
        "atom_near": set_ends(jax.random.randint(key_of[6], (NBT, NAT), 0, 3 * ATOM_DEV * N_DEV), jax.random.fold_in(key_of[6], 1), 0, (3 * ATOM_DEV * N_DEV) - 1).astype(jnp.int32),
        "harmonics": scatter_about(key_of[7], (NBT, NAT, LM, PTS), 1.0, 6.0, ((0, 512),)),
        "partition": jnp.clip(jnp.exp(math.log(0.05) - 3.218876 * jax.random.uniform(key_of[8], (NBT, NAT, PTS), jnp.float32) ** block_levels(key_of[8], (NBT, NAT, PTS), ((0, 512),), -0.2, 0.2)), 0.002, 0.05),
        "radius": jnp.clip(15.0 * jax.random.uniform(key_of[9], (NBT, NAT, PTS), jnp.float32) ** block_levels(key_of[9], (NBT, NAT, PTS), ((0, 512),), -0.2, 0.2), 0.0, 15.0),
        "radial_table": scatter_about(key_of[10], (LM, NR), 0.1, 1.5, (), jnp.float32),
    }


def spline_basis(radii_row, knot_count):
    knot_points = jnp.arange(knot_count).astype(jnp.float32)
    distance = jnp.abs(radii_row[..., None, :] - knot_points[:, None])
    inner_part = 2.0 / 3.0 - distance * distance + 0.5 * distance * distance * distance
    remote = 2.0 - distance
    outer_part = remote * remote * remote / 6.0
    return jnp.where(distance < 1.0, inner_part, jnp.where(distance < 2.0, outer_part, 0.0))


def batch_density(values, row_blocks):
    block_total = values.shape[0]
    band_width = row_blocks.shape[1]
    leading = jnp.zeros((1,) + values.shape[1:], values.dtype)
    trailing = jnp.zeros((band_width - 2,) + values.shape[1:], values.dtype)
    padded = jnp.concatenate([leading, values, trailing], axis=0)
    stacked = jnp.stack([padded[column:column + block_total] for column in range(band_width)], axis=2)
    mixed_rows = jnp.einsum("jpkf,jkgf->jpg", stacked.astype(jnp.float32), row_blocks.astype(jnp.float32), precision=lax.Precision.HIGHEST)
    return jnp.sum(values.astype(jnp.float32) * mixed_rows, axis=(0, 2))


def reference(basis_values, density_rows, block_mask, window_start, batch_offsets, batch_sizes, atom_near, harmonics, partition, radius, radial_table):
    block_count = BLK_DEV * N_DEV
    atom_region = ATOM_DEV * N_DEV
    masked = density_rows * block_mask.astype(jnp.bfloat16)[:, :, None, None]
    batch_total = basis_values.shape[0]
    device_of = jnp.arange(batch_total, dtype=jnp.int32) // BATCH_DEV
    region_of = device_of // N_DEV
    first_block = window_start[device_of] + batch_offsets.reshape(-1)
    alive_mask = (jnp.arange(PTS, dtype=jnp.int32)[None, :] < batch_sizes.reshape(-1)[:, None]).astype(jnp.float32)

    def one_density(batch_item):
        values, start_block, region_index = batch_item
        spatial = (start_block + jnp.arange(NNB, dtype=jnp.int32)) % block_count
        stored = region_index * block_count + (spatial % N_DEV) * BLK_DEV + spatial // N_DEV
        row_blocks = jnp.take(masked, stored.astype(jnp.int32), axis=0)
        return batch_density(values, row_blocks)

    density = lax.map(one_density, (basis_values, first_block, region_of)) * alive_mask

    def one_terms(batch_item):
        weights, dens_row, harmonic = batch_item
        return jnp.einsum("ip,ilp->il", weights * dens_row[None, :], harmonic.astype(jnp.float32), precision=lax.Precision.HIGHEST)

    moment_terms = lax.map(one_terms, (partition, density, harmonics))
    near_region = (region_of[:, None] + atom_near // atom_region - 1) % N_REGION
    target = (near_region * atom_region + atom_near % atom_region).astype(jnp.int32)
    summed = jax.ops.segment_sum(moment_terms.reshape(-1, moment_terms.shape[-1]), target.reshape(-1), num_segments=ATOMS)
    moments = summed.T
    spline_table = (summed[:, :, None] * radial_table[None, :, :]).astype(jnp.bfloat16)

    def one_potential(batch_item):
        selected, harmonic, radii_row = batch_item
        rows_here = jnp.take(spline_table, selected, axis=0).astype(jnp.float32)
        spline = spline_basis(radii_row, NR)
        radial = jnp.einsum("ilr,irp->ilp", rows_here, spline, precision=lax.Precision.HIGHEST)
        return jnp.sum(harmonic.astype(jnp.float32) * radial, axis=(0, 1))

    potential = lax.map(one_potential, (target, harmonics, radius)) * alive_mask
    return (density, moments, potential)
```

```python
import functools

import jax
import jax.numpy as jnp
from jax import lax
from jax.experimental import pallas as pl
from jax.experimental.pallas import tpu as pltpu
from jax.sharding import PartitionSpec as P

ATOM_DEV = 16
NX = 4
MESH = pl.DeviceIdType.MESH
NT = (((1,), (1,)), ((), ()))


def place():
    me = lax.axis_index("dev")
    return me % NX, me // NX


def remote(src, dst, send_sem, recv_sem, where):
    return pltpu.make_async_remote_copy(
        src_ref=src,
        dst_ref=dst,
        send_sem=send_sem,
        recv_sem=recv_sem,
        device_id=where,
        device_id_type=MESH,
    )


def greet(peers):
    barrier = pltpu.get_barrier_semaphore()
    for peer in peers:
        pl.semaphore_signal(barrier, inc=1, device_id=peer, device_id_type=MESH)
    pl.semaphore_wait(barrier, len(peers))


def rows_kernel(
    ny,
    rows_ref,
    mask_ref,
    meta_ref,
    win_ref,
    metas_ref,
    own,
    hold,
    out_r,
    out_l,
    out_o,
    out_me,
    relay_l,
    relay_r,
    metas,
    ys,
    yr,
    ms,
    mr,
    rs,
    ls,
    os_,
    fr,
    fl,
    fo,
    frl,
    frr,
    fws,
    local,
):
    x, y = place()
    far = ny // 2
    right = {"dev": y * NX + (x + 1) % NX}
    left = {"dev": y * NX + (x + NX - 1) % NX}
    other = {"dev": y * NX + (x + 2) % NX}
    up = {"dev": ((y + 1) % ny) * NX + x}
    down = {"dev": ((y + ny - 1) % ny) * NX + x}
    slots, band = rows_ref.shape[:2]
    for t in range(slots):
        for k in range(band):
            own[t, k] = rows_ref[t, k] * mask_ref[t * band + k]
    greet((right, left, other, up, down))
    started = []

    def go(copy):
        copy.start()
        started.append(copy)

    go(remote(own, hold.at[0], ys.at[0], yr.at[0], down))
    go(remote(own, hold.at[far], ys.at[far], yr.at[far], up))
    mine = pltpu.make_async_copy(meta_ref, metas.at[0, x], local.at[0])
    mine.start()
    for i, peer in enumerate((right, left, other)):
        go(remote(meta_ref, metas.at[0, x], ms.at[i], mr.at[i], peer))

    def meta_in(i, xx):
        remote(meta_ref, metas.at[0, xx], ms.at[i], mr.at[i], right).wait_recv()

    xr, xl, xo = (x + 1) % NX, (x + NX - 1) % NX, (x + 2) % NX
    meta_in(0, xl)
    meta_in(1, xr)
    meta_in(2, xo)
    mine.wait()
    base = 3
    go(remote(metas.at[0], metas.at[1], ms.at[base], mr.at[base], down))
    go(remote(metas.at[0], metas.at[ny - 1], ms.at[base + far], mr.at[base + far], up))

    order = [0]
    for s in range(1, far + 1):
        order.append(s)
        if s < far:
            order.append(-s)

    def weights(xx, d):
        q = metas[0, xx, 1:2, :]
        m = metas[0, xx, 2:3, :]
        slot = q + jnp.where(m > d, 1, 0)
        slot = jnp.where(slot >= slots, slot - slots, slot)
        return [
            jnp.where(slot == t, 1.0, 0.0).astype(jnp.float32).astype(jnp.bfloat16)
            for t in range(slots)
        ]

    def process(g):
        rho = order[g]
        yy = (y + rho + ny) % ny
        d = yy * NX + x
        source = own if rho == 0 else hold.at[rho - 1 if rho > 0 else far - rho - 1]
        picks = [(xx, dst, weights(xx, d)) for xx, dst in ((xr, out_r), (xl, out_l), (xo, out_o), (x, out_me))]

        def one(k, carry):
            parts = [source[t, k] for t in range(slots)]
            for _, dst, w in picks:
                total = parts[0] * w[0]
                for t in range(1, slots):
                    total = total + parts[t] * w[t]
                dst[g, k] = total
            return carry

        lax.fori_loop(0, band, one, 0)
        go(remote(out_r.at[g], win_ref.at[d], rs.at[g], fl.at[g], right))
        go(remote(out_l.at[g], win_ref.at[d], ls.at[g], fr.at[g], left))
        if g % 2 == 0:
            go(remote(out_o.at[g], relay_l.at[g // 2], os_.at[g], frl.at[g // 2], right))
        else:
            go(remote(out_o.at[g], relay_r.at[g // 2], os_.at[g], frr.at[g // 2], left))
        copy = pltpu.make_async_copy(out_me.at[g], win_ref.at[d], local.at[1 + g])
        copy.start()
        return copy

    def passing(g):
        yy = (y + order[g] + ny) % ny
        i = g // 2
        if g % 2 == 0:
            remote(out_o.at[g], relay_l.at[i], os_.at[g], frl.at[i], right).wait_recv()
            go(remote(relay_l.at[i], win_ref.at[yy * NX + xl], fws.at[g], fo.at[g], right))
        else:
            remote(out_o.at[g], relay_r.at[i], os_.at[g], frr.at[i], left).wait_recv()
            go(remote(relay_r.at[i], win_ref.at[yy * NX + xr], fws.at[g], fo.at[g], left))

    kept = [process(0)]
    done = 0
    for s in range(1, far + 1):
        i = s - 1
        remote(own, hold.at[i], ys.at[i], yr.at[i], down).wait_recv()
        remote(metas.at[0], metas.at[s], ms.at[base + i], mr.at[base + i], down).wait_recv()
        if s < far:
            go(remote(hold.at[i], hold.at[i + 1], ys.at[i + 1], yr.at[i + 1], down))
            go(remote(metas.at[s], metas.at[s + 1], ms.at[base + i + 1], mr.at[base + i + 1], down))
        if s < far:
            j = far + i
            remote(own, hold.at[j], ys.at[j], yr.at[j], up).wait_recv()
            remote(metas.at[0], metas.at[ny - s], ms.at[base + j], mr.at[base + j], up).wait_recv()
            if s < far - 1:
                go(remote(hold.at[j], hold.at[j + 1], ys.at[j + 1], yr.at[j + 1], up))
                go(remote(metas.at[ny - s], metas.at[ny - s - 1], ms.at[base + j + 1], mr.at[base + j + 1], up))
        kept.append(process(2 * s - 1))
        if s < far:
            kept.append(process(2 * s))
        upto = 2 * s - 1
        while done < upto:
            passing(done)
            done += 1
    while done < ny:
        passing(done)
        done += 1
    metas_out = []
    for rho in range(ny):
        copy = pltpu.make_async_copy(metas.at[rho], metas_ref.at[(y + rho) % ny], local.at[1 + ny + rho])
        copy.start()
        metas_out.append(copy)
    for g in range(ny):
        yy = (y + order[g] + ny) % ny
        remote(out_r.at[g], win_ref.at[yy * NX + xl], rs.at[g], fl.at[g], right).wait_recv()
        remote(out_l.at[g], win_ref.at[yy * NX + xr], ls.at[g], fr.at[g], left).wait_recv()
        remote(out_o.at[g], win_ref.at[yy * NX + xo], fws.at[g], fo.at[g], right).wait_recv()
    for copy in started:
        copy.wait_send()
    for copy in kept + metas_out:
        copy.wait()


def gather_rows(rows, mask, meta, ny):
    slots, band, size, _ = rows.shape
    count = ny * NX
    bf, dma = jnp.bfloat16, pltpu.SemaphoreType.DMA
    half = (ny + 1) // 2
    vm = pl.BlockSpec(memory_space=pltpu.VMEM)
    block = (band, size, size)
    return pl.pallas_call(
        functools.partial(rows_kernel, ny),
        name="gather_rows",
        out_shape=(
            jax.ShapeDtypeStruct((count,) + block, bf),
            jax.ShapeDtypeStruct((ny, NX) + meta.shape, jnp.int32),
        ),
        in_specs=[vm, vm, vm],
        out_specs=(pl.BlockSpec(memory_space=pl.ANY), pl.BlockSpec(memory_space=pl.ANY)),
        scratch_shapes=[
            pltpu.VMEM((slots,) + block, bf),
            pltpu.VMEM((ny - 1, slots) + block, bf),
            pltpu.VMEM((ny,) + block, bf),
            pltpu.VMEM((ny,) + block, bf),
            pltpu.VMEM((ny,) + block, bf),
            pltpu.VMEM((ny,) + block, bf),
            pltpu.VMEM((half,) + block, bf),
            pltpu.VMEM((half,) + block, bf),
            pltpu.VMEM((ny, NX) + meta.shape, jnp.int32),
            dma((ny,)),
            dma((ny,)),
            dma((ny + 3,)),
            dma((ny + 3,)),
            dma((ny,)),
            dma((ny,)),
            dma((ny,)),
            dma((ny,)),
            dma((ny,)),
            dma((ny,)),
            dma((half,)),
            dma((half,)),
            dma((ny,)),
            dma((2 * ny + 1,)),
        ],
        compiler_params=pltpu.CompilerParams(collective_id=0, has_side_effects=True),
    )(rows, mask, meta)


def density_kernel(start, offsets, sizes, win_ref, basis_ref, harm_ref, part_ref, dens_ref, terms_ref):
    b = pl.program_id(0)
    count = win_ref.shape[0]
    size = win_ref.shape[2]
    near, comps, points = harm_ref.shape[1:]

    @pl.when(b == 0)
    def _():
        terms_ref[...] = jnp.zeros_like(terms_ref)

    first = start[0] + offsets[b]
    places = [lax.rem(first + j, count) for j in range(4)]

    def piece(j, k):
        return win_ref[places[j], k]

    v = [basis_ref[0, j] for j in range(4)]
    v01 = jnp.concatenate([v[0], v[1]], axis=1)
    v23 = jnp.concatenate([v[2], v[3]], axis=1)

    def quad(a, b_, c, d):
        return jnp.concatenate([jnp.concatenate([a, b_], axis=1), jnp.concatenate([c, d], axis=1)], axis=0)

    zero = jnp.zeros((size, size), jnp.bfloat16)
    dot = functools.partial(lax.dot_general, dimension_numbers=NT, preferred_element_type=jnp.float32)
    m01 = dot(v01, quad(piece(0, 1), piece(0, 2), piece(1, 0), piece(1, 1)))
    m01 = m01 + dot(v23, quad(piece(0, 3), zero, piece(1, 2), piece(1, 3)))
    m23 = dot(v23, quad(piece(2, 1), piece(2, 2), piece(3, 0), piece(3, 1)))
    m2x = dot(v[1], piece(2, 0))
    f32 = jnp.float32
    total = v[0].astype(f32) * m01[:, :size] + v[1].astype(f32) * m01[:, size:]
    total = total + v[2].astype(f32) * (m23[:, :size] + m2x) + v[3].astype(f32) * m23[:, size:]
    row = jnp.sum(total.T, axis=0, keepdims=True)
    lane = lax.broadcasted_iota(jnp.int32, (1, points), 1)
    row = jnp.where(lane < sizes[b], row, 0.0)
    dens_ref[0] = row
    weight = part_ref[0] * row
    spot = lax.broadcasted_iota(jnp.int32, (comps, 128), 1)
    gained = terms_ref[0:comps, :]
    for i in range(near):
        column = jnp.sum(harm_ref[0, i].astype(f32) * weight[i : i + 1, :], axis=1, keepdims=True)
        gained = jnp.where(spot == b * near + i, column, gained)
    terms_ref[0:comps, :] = gained


def densities(start, offsets, sizes, win, basis, harm, part):
    batches, nnb, points, size = basis.shape
    near, comps = harm.shape[1:3]
    return pl.pallas_call(
        density_kernel,
        name="densities",
        out_shape=(
            jax.ShapeDtypeStruct((batches, 1, points), jnp.float32),
            jax.ShapeDtypeStruct((32, 128), jnp.float32),
        ),
        grid_spec=pltpu.PrefetchScalarGridSpec(
            num_scalar_prefetch=3,
            grid=(batches,),
            in_specs=[
                pl.BlockSpec(win.shape, lambda b, *_: (0, 0, 0, 0), pipeline_mode=pl.Buffered(1)),
                pl.BlockSpec((1, nnb, points, size), lambda b, *_: (b, 0, 0, 0)),
                pl.BlockSpec((1, near, comps, points), lambda b, *_: (b, 0, 0, 0)),
                pl.BlockSpec((1, near, points), lambda b, *_: (b, 0, 0)),
            ],
            out_specs=(
                pl.BlockSpec((1, 1, points), lambda b, *_: (b, 0, 0)),
                pl.BlockSpec((32, 128), lambda b, *_: (0, 0)),
            ),
        ),
    )(start, offsets, sizes, win, basis, harm, part)


def moments_kernel(
    ny,
    terms_ref,
    metas_ref,
    out_ref,
    outt_ref,
    every,
    asked,
    hot,
    split,
    answer,
    got,
    ysend,
    yrecv,
    xsend,
    xrecv,
    qsend,
    qrecv,
    zsend,
    zrecv,
    local,
):
    x, y = place()
    region = lax.axis_index("region")
    regions = lax.axis_size("region")
    me = y * NX + x
    ups = [{"dev": ((y + s) % ny) * NX + x} for s in range(1, ny)]
    sides = [{"dev": y * NX + (x + s) % NX} for s in range(1, NX)]
    hops = (1, 2, -1, -2)
    nears = [{"region": (region + h + regions) % regions} for h in hops]
    greet(ups + sides + nears)
    started = []

    def go(copy):
        copy.start()
        started.append(copy)

    for i, s in enumerate(range(1, ny)):
        go(remote(terms_ref, every.at[y, x], ysend.at[i], yrecv.at[i], ups[i]))
    for i in range(len(hops)):
        go(remote(metas_ref.at[y, x], asked.at[i], qsend.at[i], qrecv.at[i], nears[i]))
    mine = pltpu.make_async_copy(terms_ref, every.at[y, x], local.at[0])
    mine.start()
    for i in range(NX - 1):
        go(remote(terms_ref, every.at[y, x], xsend.at[0, i], xrecv.at[0, i], sides[i]))

    def spread(j):
        yy = (y + ny - j) % ny
        remote(terms_ref, every.at[yy, x], ysend.at[j - 1], yrecv.at[j - 1], ups[0]).wait_recv()
        for i in range(NX - 1):
            go(remote(every.at[yy, x], every.at[yy, x], xsend.at[j, i], xrecv.at[j, i], sides[i]))

    near_first = sorted(range(1, ny), key=lambda j: min(j, ny - j))
    count = ny * NX

    def fill(slot, line):
        column = jnp.broadcast_to(line, (128, 128)).T

        def one(t, carry):
            target = metas_ref[t // NX, t % NX, 0:1, :]
            same = jnp.where(column == target, 1.0, 0.0).astype(jnp.float32)
            hot[t, slot * 128 : (slot + 1) * 128, :] = same.astype(jnp.bfloat16)
            return carry

        lax.fori_loop(0, count, one, 0)

    for j in near_first[:2]:
        spread(j)
    fill(0, metas_ref[y, x, 0:1, :])
    for j in near_first[2:4]:
        spread(j)
    for i in range(len(hops)):
        remote(metas_ref.at[y, x], asked.at[i], qsend.at[i], qrecv.at[i], nears[0]).wait_recv()
    fill(1, asked[0, 0:1, :])
    for j in near_first[4:]:
        spread(j)
    for i in range(1, len(hops)):
        fill(1 + i, asked[i, 0:1, :])
    mine.wait()
    for j in range(ny):
        yy = (y + ny - j) % ny
        for i in range(NX - 1):
            xx = (x + NX - 1 - i) % NX
            remote(terms_ref, every.at[yy, xx], xsend.at[j, i], xrecv.at[j, i], sides[0]).wait_recv()

    def parts(t, carry):
        value = every[t // NX, t % NX]
        high = value.astype(jnp.bfloat16)
        split[t, 0:32, :] = high
        split[t, 32:64, :] = (value - high.astype(jnp.float32)).astype(jnp.bfloat16)
        return carry

    lax.fori_loop(0, count, parts, 0)

    def add(t, total):
        left = jnp.concatenate([split[2 * t], split[2 * t + 1]], axis=1)
        right = jnp.concatenate([hot[2 * t], hot[2 * t + 1]], axis=1)
        return total + lax.dot_general(left, right, NT, preferred_element_type=jnp.float32)

    width = 128 * (1 + len(hops))
    sums = lax.fori_loop(0, count // 2, add, jnp.zeros((64, width), jnp.float32))
    sums = sums[0:32, :] + sums[32:64, :]
    for i in range(len(hops)):
        answer[i] = sums[:, 128 * (i + 1) : 128 * (i + 2)]
    for i in range(len(hops)):
        back = {"region": (region - hops[i] + regions) % regions}
        go(remote(answer.at[i], got.at[i], zsend.at[i], zrecv.at[i], back))
    whole = sums[:, 0:128]
    for i in range(len(hops)):
        remote(answer.at[i], got.at[i], zsend.at[i], zrecv.at[i], nears[0]).wait_recv()
        whole = whole + got[i]
    out_ref[...] = whole
    outt_ref[...] = jnp.concatenate([whole, jnp.zeros((96, 128), jnp.float32)], axis=0).T
    for copy in started:
        copy.wait_send()


def sum_moments(terms, metas, ny):
    count = ny * NX
    dma = pltpu.SemaphoreType.DMA
    vm = pl.BlockSpec(memory_space=pltpu.VMEM)
    f32, bf = jnp.float32, jnp.bfloat16
    return pl.pallas_call(
        functools.partial(moments_kernel, ny),
        name="sum_moments",
        out_shape=(jax.ShapeDtypeStruct((32, 128), f32), jax.ShapeDtypeStruct((128, 128), f32)),
        in_specs=[vm, vm],
        out_specs=(vm, vm),
        scratch_shapes=[
            pltpu.VMEM((ny, NX, 32, 128), f32),
            pltpu.VMEM((4,) + metas.shape[2:], jnp.int32),
            pltpu.VMEM((count, 640, 128), bf),
            pltpu.VMEM((count, 64, 128), bf),
            pltpu.VMEM((4, 32, 128), f32),
            pltpu.VMEM((4, 32, 128), f32),
            dma((ny - 1,)),
            dma((ny - 1,)),
            dma((ny, NX - 1)),
            dma((ny, NX - 1)),
            dma((4,)),
            dma((4,)),
            dma((4,)),
            dma((4,)),
            dma((1,)),
        ],
        compiler_params=pltpu.CompilerParams(collective_id=1, has_side_effects=True),
    )(terms, metas)


def potential_kernel(sizes, moments_ref, radial_ref, harm_ref, radius_ref, pot_ref):
    b = pl.program_id(0)
    near, comps, points = harm_ref.shape[1:]
    knots = radial_ref.shape[0]
    f32 = jnp.float32
    knot = lax.broadcasted_iota(jnp.int32, (knots, points), 0).astype(f32)
    total = jnp.zeros((knots, points), f32)
    for i in range(near):
        moment = moments_ref[pl.ds(b * near + i, 1), 0:comps]
        table = (moment * radial_ref[...]).astype(jnp.bfloat16)
        mixed = jnp.dot(table, harm_ref[0, i], preferred_element_type=f32)
        distance = jnp.abs(radius_ref[0, i : i + 1, :] - knot)
        inner = 2.0 / 3.0 - distance * distance + 0.5 * distance * distance * distance
        remote_ = 2.0 - distance
        outer = remote_ * remote_ * remote_ * (1.0 / 6.0)
        spline = jnp.where(distance < 1.0, inner, jnp.where(distance < 2.0, outer, 0.0))
        total = total + mixed * spline
    row = jnp.sum(total, axis=0, keepdims=True)
    lane = lax.broadcasted_iota(jnp.int32, (1, points), 1)
    pot_ref[0] = jnp.where(lane < sizes[b], row, 0.0)


def potentials(sizes, moments, radial, harm, radius):
    batches, near, comps, points = harm.shape
    return pl.pallas_call(
        potential_kernel,
        name="potentials",
        out_shape=jax.ShapeDtypeStruct((batches, 1, points), jnp.float32),
        grid_spec=pltpu.PrefetchScalarGridSpec(
            num_scalar_prefetch=1,
            grid=(batches,),
            in_specs=[
                pl.BlockSpec(moments.shape, lambda b, *_: (0, 0)),
                pl.BlockSpec(radial.shape, lambda b, *_: (0, 0)),
                pl.BlockSpec((1, near, comps, points), lambda b, *_: (b, 0, 0, 0)),
                pl.BlockSpec((1, near, points), lambda b, *_: (b, 0, 0)),
            ],
            out_specs=pl.BlockSpec((1, 1, points), lambda b, *_: (b, 0, 0)),
        ),
    )(sizes, moments, radial, harm, radius)


def per_device(
    basis_values,
    density_rows,
    block_mask,
    window_start,
    batch_offsets,
    batch_sizes,
    atom_near,
    harmonics,
    partition,
    radius,
    radial_table,
):
    devs = lax.axis_size("dev")
    regions = lax.axis_size("region")
    ny = devs // NX
    me, region = lax.axis_index("dev"), lax.axis_index("region")
    atom_region = ATOM_DEV * devs
    batches, near = atom_near.shape
    pairs = batches * near
    comps = radial_table.shape[0]
    flat = atom_near.reshape(pairs)
    target = lax.rem(region + flat // atom_region - 1 + regions, regions) * atom_region + flat % atom_region
    owned = region * atom_region + me * ATOM_DEV + jnp.arange(ATOM_DEV, dtype=jnp.int32)
    line = jnp.concatenate([target, owned, jnp.full((128 - pairs - ATOM_DEV,), -1, jnp.int32)])
    start = window_start[0]
    meta = jnp.stack(
        [
            line,
            jnp.full((128,), start // devs, jnp.int32),
            jnp.full((128,), start % devs, jnp.int32),
            jnp.zeros((128,), jnp.int32),
        ]
    )
    mask = jnp.broadcast_to(block_mask.reshape(-1)[:, None, None], (block_mask.size, 1, 128)).astype(jnp.bfloat16)
    win, metas = gather_rows(density_rows, mask, meta, ny)
    density, terms = densities(
        window_start, batch_offsets[0], batch_sizes[0], win, basis_values, harmonics, partition
    )
    sums, sums_t = sum_moments(terms, metas, ny)
    moments = sums[:comps, pairs : pairs + ATOM_DEV]
    potential = potentials(batch_sizes[0], sums_t, radial_table.T, harmonics, radius)
    points = basis_values.shape[2]
    return (density.reshape(batches, points), moments, potential.reshape(batches, points))


def solution(mesh):
    placed = (
        P(("region", "dev"), None, None, None),
        P(("region", "dev"), None, None, None),
        P(("region", "dev"), None),
        P(("region", "dev")),
        P(("region", "dev"), None),
        P(("region", "dev"), None),
        P(("region", "dev"), None),
        P(("region", "dev"), None, None, None),
        P(("region", "dev"), None, None),
        P(("region", "dev"), None, None),
        P(),
    )
    return jax.shard_map(
        per_device,
        mesh=mesh,
        in_specs=placed,
        out_specs=(
            P(("region", "dev"), None),
            P(None, ("region", "dev")),
            P(("region", "dev"), None),
        ),
        check_vma=False,
    )
```

```python
import functools

import jax
import jax.numpy as jnp
from jax import lax
from jax.experimental import pallas as pl
from jax.experimental.pallas import tpu as pltpu
from jax.sharding import PartitionSpec as P

ATOM_DEV = 16
NX = 4
CHUNKS = 4
HOPS = (1, 2, -1, -2)
MESH = pl.DeviceIdType.MESH
NT = (((1,), (1,)), ((), ()))
TN = (((0,), (0,)), ((), ()))
F32, BF = jnp.float32, jnp.bfloat16


def remote(src, dst, send_sem, recv_sem, where):
    return pltpu.make_async_remote_copy(
        src_ref=src,
        dst_ref=dst,
        send_sem=send_sem,
        recv_sem=recv_sem,
        device_id=where,
        device_id_type=MESH,
    )


def spline_values(radii, knots):
    knot = lax.broadcasted_iota(jnp.int32, (knots, radii.shape[1]), 0).astype(F32)
    distance = jnp.abs(radii - knot)
    inner = 2.0 / 3.0 - distance * distance + 0.5 * distance * distance * distance
    rest = 2.0 - distance
    outer = rest * rest * rest * (1.0 / 6.0)
    return jnp.where(distance < 1.0, inner, jnp.where(distance < 2.0, outer, 0.0))


def pack(terms, pairs):
    lane = lax.broadcasted_iota(jnp.int32, (8, 128), 1)
    row = lax.broadcasted_iota(jnp.int32, (8, 128), 0)
    third = terms[16:24]
    last = jnp.broadcast_to(terms[24:25], (8, 128))
    top = jnp.where(lane < pairs, terms[0:8], pltpu.roll(third, 72, 1))
    tail = jnp.where(row == 0, pltpu.roll(last, 88, 1), jnp.where(row == 1, pltpu.roll(last, 48, 1), 0.0))
    low = jnp.where(lane < pairs, terms[8:16], jnp.where(lane < 88, pltpu.roll(third, 16, 1), tail))
    return top, low


def unpack(top, low, pairs):
    lane = lax.broadcasted_iota(jnp.int32, (8, 128), 1)
    row = lax.broadcasted_iota(jnp.int32, (8, 128), 0)
    live = lane < pairs
    first = jnp.where(live, top, 0.0)
    second = jnp.where(live, low, 0.0)
    third = jnp.where(lane < 56, pltpu.roll(top, 56, 1), jnp.where(live, pltpu.roll(low, 112, 1), 0.0))
    zero = jnp.broadcast_to(low[0:1], (8, 128))
    one = jnp.broadcast_to(low[1:2], (8, 128))
    last = jnp.where(lane < 40, pltpu.roll(zero, 40, 1), jnp.where(live, pltpu.roll(one, 80, 1), 0.0))
    last = jnp.where(row == 0, last, 0.0)
    return jnp.concatenate([first, second, third, last], axis=0)


def kernel(
    ny,
    rows_ref,
    mask_ref,
    start_ref,
    offsets_ref,
    sizes_ref,
    near_ref,
    part_ref,
    radius_ref,
    radial_ref,
    basis_hbm,
    harm_hbm,
    dens_ref,
    mom_ref,
    pot_ref,
    own,
    hold,
    out_r,
    out_l,
    out_o,
    relay,
    win,
    line,
    metas,
    asked,
    basis,
    harm,
    turned,
    parted,
    radial,
    packed,
    every,
    hot,
    sums,
    answer,
    got,
    ys,
    yr,
    ms,
    mr,
    qs,
    qr,
    rs,
    ls,
    os_,
    fr,
    fl,
    fo,
    frel,
    fws,
    ts,
    tr,
    xs,
    xr_,
    zs,
    zr,
    local,
):
    region, me = lax.axis_index("region"), lax.axis_index("dev")
    regions, devs = lax.axis_size("region"), ny * NX
    x, y = me % NX, me // NX
    far = ny // 2
    xr, xl, xo = (x + 1) % NX, (x + NX - 1) % NX, (x + 2) % NX
    right, left, other = ({"dev": y * NX + xx} for xx in (xr, xl, xo))
    ups = [{"dev": ((y + s) % ny) * NX + x} for s in range(1, ny)]
    up, down = ups[0], ups[-1]
    nears = [{"region": (region + h + regions) % regions} for h in HOPS]
    slots, band, size, _ = rows_ref.shape
    step = band // CHUNKS
    near, batches = near_ref.shape
    pairs = near * batches
    knots, comps = radial_ref.shape
    points = part_ref.shape[2]
    started = []

    def go(copy):
        copy.start()
        started.append(copy)

    barrier = pltpu.get_barrier_semaphore()
    greeted = ups + [right, left, other] + nears
    for peer in greeted:
        pl.semaphore_signal(barrier, inc=1, device_id=peer, device_id_type=MESH)
    fetch_basis = pltpu.make_async_copy(basis_hbm, basis, local.at[0])
    fetch_basis.start()
    fetch_harm = pltpu.make_async_copy(harm_hbm, harm, local.at[1])
    fetch_harm.start()

    for t in range(slots):
        for k in range(band):
            keep = jnp.full((1, 1), mask_ref[t, k], jnp.int32).astype(F32).astype(BF)
            own[k, t] = rows_ref[t, k] * keep

    lane = lax.broadcasted_iota(jnp.int32, (1, 128), 1)
    line[...] = jnp.zeros_like(line)
    line[0:near, 0:batches] = near_ref[...]
    total = jnp.zeros((1, 128), jnp.int32)
    for i in range(near):
        moved = pltpu.roll(jnp.broadcast_to(line[i : i + 1, :], (8, 128)), i * batches, 1)[0:1]
        total = jnp.where((lane >= i * batches) & (lane < (i + 1) * batches), moved, total)
    atom_region = ATOM_DEV * devs
    bits = atom_region.bit_length() - 1
    side = region + lax.shift_right_logical(total, bits) - 1
    side = jnp.where(side < 0, side + regions, jnp.where(side >= regions, side - regions, side))
    target = side * atom_region + (total & (atom_region - 1))
    owned = region * atom_region + me * ATOM_DEV + lane - pairs
    whole_line = jnp.where(lane < pairs, target, jnp.where(lane < pairs + ATOM_DEV, owned, -1))
    start = start_ref[0]
    line[0:1] = whole_line
    line[1:2] = jnp.full((1, 128), start // devs, jnp.int32)
    line[2:3] = jnp.full((1, 128), start % devs, jnp.int32)
    metas[0, x] = line[0:4]
    pl.semaphore_wait(barrier, len(greeted))

    def part_of(ref, c):
        return ref.at[pl.ds(c * step, step)]

    for c in range(CHUNKS):
        go(remote(part_of(own, c), part_of(hold.at[0], c), ys.at[0, c], yr.at[0, c], down))
        go(remote(part_of(own, c), part_of(hold.at[far], c), ys.at[far, c], yr.at[far, c], up))
        if c == 0:
            for i, peer in enumerate((right, left, other)):
                go(remote(line.at[0:4], metas.at[0, x], ms.at[i], mr.at[i], peer))
    for i in range(len(HOPS)):
        go(remote(line.at[0:4], asked.at[i], qs.at[i], qr.at[i], nears[i]))

    for i, xx in enumerate((xl, xr, xo)):
        remote(line.at[0:4], metas.at[0, xx], ms.at[i], mr.at[i], right).wait_recv()
    base = 3
    go(remote(metas.at[0], metas.at[1], ms.at[base], mr.at[base], down))
    go(remote(metas.at[0], metas.at[ny - 1], ms.at[base + far], mr.at[base + far], up))

    order = [0]
    for s in range(1, far + 1):
        order.append(s)
        if s < far:
            order.append(-s)

    def row_of(g):
        return (y + order[g] + ny) % ny

    def weights(xx, d):
        q = metas[0, xx, 1:2, :]
        m = metas[0, xx, 2:3, :]
        slot = q + jnp.where(m > d, 1, 0)
        slot = jnp.where(slot >= slots, slot - slots, slot)
        return [jnp.where(slot == t, 1.0, 0.0).astype(F32).astype(BF) for t in range(slots)]

    def via_right(g, c):
        return (g + c) % 2 == 0

    def process(g, c):
        rho = order[g]
        d = row_of(g) * NX + x
        source = own if rho == 0 else hold.at[rho - 1 if rho > 0 else far - rho - 1]
        picks = [(dst, weights(xx, d)) for xx, dst in ((xr, out_r.at[g]), (xl, out_l.at[g]), (xo, out_o.at[g]), (x, win.at[d]))]
        for k in range(c * step, (c + 1) * step):
            parts = [source[k, t] for t in range(slots)]
            for dst, w in picks:
                chosen = parts[0] * w[0]
                for t in range(1, slots):
                    chosen = chosen + parts[t] * w[t]
                dst[k] = chosen
        go(remote(part_of(out_o.at[g], c), part_of(relay.at[g], c), os_.at[g, c], frel.at[g, c], right if via_right(g, c) else left))
        go(remote(part_of(out_r.at[g], c), part_of(win.at[d], c), rs.at[g, c], fl.at[g, c], right))
        go(remote(part_of(out_l.at[g], c), part_of(win.at[d], c), ls.at[g, c], fr.at[g, c], left))

    def passing(g, c):
        toward, origin = (right, xl) if via_right(g, c) else (left, xr)
        d = row_of(g) * NX + origin
        remote(part_of(out_o.at[g], c), part_of(relay.at[g], c), os_.at[g, c], frel.at[g, c], right).wait_recv()
        go(remote(part_of(relay.at[g], c), part_of(win.at[d], c), fws.at[g, c], fo.at[g, c], toward))

    def prepare(b, carry):
        for j in range(band):
            turned[b, j * size : (j + 1) * size, :] = basis[b, j].T
        for i in range(near):
            values = harm[b, i].astype(F32)
            parted[b, i] = values * part_ref[b, i : i + 1, :]
            spline = spline_values(radius_ref[b, i : i + 1, :], knots)
            curve = lax.dot_general(
                radial_ref[...], spline, TN, precision=lax.Precision.HIGHEST, preferred_element_type=F32
            )
            radial[b, i] = values * curve
        return carry

    def fill(slot, asked_line):
        column = jnp.broadcast_to(asked_line, (128, 128)).T

        def one(t, carry):
            r = lax.rem(t // NX + ny - y, ny)
            wanted = metas[r, t % NX, 0:1, :]
            same = jnp.where(column == wanted, 1.0, 0.0).astype(F32)
            hot[t, slot * 128 : (slot + 1) * 128, :] = same.astype(BF)
            return carry

        lax.fori_loop(0, devs, one, 0)

    for c in range(CHUNKS):
        process(0, c)
    fetch_basis.wait()
    fetch_harm.wait()
    per = -(-batches // (CHUNKS * (far - 1)))
    ready = 0
    lag = []
    for s in range(1, far + 1):
        i, j = s - 1, far + s - 1
        for c in range(CHUNKS):
            remote(part_of(own, c), part_of(hold.at[i], c), ys.at[i, c], yr.at[i, c], down).wait_recv()
            if s < far:
                go(remote(part_of(hold.at[i], c), part_of(hold.at[i + 1], c), ys.at[i + 1, c], yr.at[i + 1, c], down))
                remote(part_of(own, c), part_of(hold.at[j], c), ys.at[j, c], yr.at[j, c], up).wait_recv()
                if s < far - 1:
                    go(remote(part_of(hold.at[j], c), part_of(hold.at[j + 1], c), ys.at[j + 1, c], yr.at[j + 1, c], up))
            if c == 0:
                remote(metas.at[0], metas.at[s], ms.at[base + i], mr.at[base + i], down).wait_recv()
                if s < far:
                    go(remote(metas.at[s], metas.at[s + 1], ms.at[base + i + 1], mr.at[base + i + 1], down))
                    remote(metas.at[0], metas.at[ny - s], ms.at[base + j], mr.at[base + j], up).wait_recv()
                    if s < far - 1:
                        go(remote(metas.at[ny - s], metas.at[ny - s - 1], ms.at[base + j + 1], mr.at[base + j + 1], up))
            process(2 * s - 1, c)
            if s < far:
                process(2 * s, c)
            if s == 1:
                lag.append((0, c))
            else:
                lag.append((2 * s - 3, c))
                lag.append((2 * s - 2, c))
            while lag:
                passing(*lag.pop(0))
            if ready < batches and s < far:
                upto = min(batches, ready + per)
                lax.fori_loop(ready, upto, prepare, 0)
                ready = upto
    for i in range(len(HOPS)):
        remote(line.at[0:4], asked.at[i], qs.at[i], qr.at[i], nears[0]).wait_recv()
    fill(0, metas[0, x, 0:1, :])
    fill(1, asked[0, 0:1, :])
    for c in range(CHUNKS):
        passing(ny - 1, c)
    for i in range(1, len(HOPS)):
        fill(1 + i, asked[i, 0:1, :])
    for g in range(ny):
        row = row_of(g) * NX
        for c in range(CHUNKS):
            remote(part_of(out_r.at[g], c), part_of(win.at[row + xl], c), rs.at[g, c], fl.at[g, c], right).wait_recv()
            remote(part_of(out_l.at[g], c), part_of(win.at[row + xr], c), ls.at[g, c], fr.at[g, c], left).wait_recv()
            remote(part_of(out_o.at[g], c), part_of(win.at[row + xo], c), fws.at[g, c], fo.at[g, c], right).wait_recv()

    zero = jnp.zeros((size, size), BF)
    wide = lax.broadcasted_iota(jnp.int32, (1, points), 1)
    spot = lax.broadcasted_iota(jnp.int32, (comps, 128), 1)

    def batch(b, gained):
        first = start + offsets_ref[0, b]
        places = [lax.rem(first + j, devs) for j in range(band)]

        def piece(j, k):
            return win[places[j], k]

        def quad(a, b_, c, d):
            return jnp.concatenate([jnp.concatenate([a, b_], axis=1), jnp.concatenate([c, d], axis=1)], axis=0)

        low, high = turned[b, 0 : 2 * size, :], turned[b, 2 * size : 4 * size, :]
        dot = functools.partial(jnp.dot, preferred_element_type=F32)
        m01 = dot(quad(piece(0, 1), piece(0, 2), piece(1, 0), piece(1, 1)), low)
        m01 = m01 + dot(quad(piece(0, 3), zero, piece(1, 2), piece(1, 3)), high)
        m23 = dot(quad(piece(2, 1), piece(2, 2), piece(3, 0), piece(3, 1)), high)
        m2x = dot(piece(2, 0), turned[b, size : 2 * size, :])
        density = jnp.sum(m01 * low.astype(F32) + m23 * high.astype(F32), axis=0, keepdims=True)
        density = density + jnp.sum(m2x * turned[b, 2 * size : 3 * size, :].astype(F32), axis=0, keepdims=True)
        density = jnp.where(wide < sizes_ref[0, b], density, 0.0)
        dens_ref[b] = density
        for i in range(near):
            column = jnp.sum(parted[b, i] * density, axis=1, keepdims=True)
            gained = jnp.where(spot == i * batches + b, column, gained)
        return gained

    terms = lax.fori_loop(0, batches, batch, jnp.zeros((comps, 128), F32))
    top, low = pack(terms, pairs)
    packed[0:8] = top
    packed[8:16] = low

    sides = [{"dev": y * NX + (x + s) % NX} for s in range(1, NX)]
    for i in range(ny - 1):
        go(remote(packed, every.at[y, x], ts.at[i], tr.at[i], ups[i]))
    for i in range(NX - 1):
        go(remote(packed, every.at[y, x], xs.at[0, i], xr_.at[0, i], sides[i]))
    every[y, x] = packed[...]
    near_first = sorted(range(1, ny), key=lambda j: min(j, ny - j))

    def spread(j):
        yy = (y + ny - j) % ny
        remote(packed, every.at[yy, x], ts.at[j - 1], tr.at[j - 1], up).wait_recv()
        for i in range(NX - 1):
            go(remote(every.at[yy, x], every.at[yy, x], xs.at[j, i], xr_.at[j, i], sides[i]))

    sums[...] = jnp.zeros_like(sums)

    def collect(j):
        yy = (y + ny - j) % ny
        for i in range(NX - 1):
            xx = (x + NX - 1 - i) % NX
            remote(packed, every.at[yy, xx], xs.at[j, i], xr_.at[j, i], right).wait_recv()
        for pair in range(NX // 2):
            lefts, rights = [], []
            for xx in (2 * pair, 2 * pair + 1):
                value = unpack(every[yy, xx, 0:8], every[yy, xx, 8:16], pairs)
                high = value.astype(BF)
                lowp = (value - high.astype(F32)).astype(BF)
                lefts.append(jnp.concatenate([high, lowp], axis=0))
                rights.append(hot[yy * NX + xx])
            sums[...] += lax.dot_general(
                jnp.concatenate(lefts, axis=1), jnp.concatenate(rights, axis=1), NT, preferred_element_type=F32
            )

    for j in near_first:
        spread(j)
    collect(0)
    for j in near_first:
        collect(j)
    both = sums[0:32, :] + sums[32:64, :]
    for i in range(len(HOPS)):
        answer[i] = both[:, 128 * (i + 1) : 128 * (i + 2)]
    for i in range(len(HOPS)):
        back = {"region": (region - HOPS[i] + regions) % regions}
        go(remote(answer.at[i], got.at[i], zs.at[i], zr.at[i], back))
    moment = both[:, 0:128]
    for i in range(len(HOPS)):
        remote(answer.at[i], got.at[i], zs.at[i], zr.at[i], nears[0]).wait_recv()
        moment = moment + got[i]
    upright = jnp.concatenate([moment, jnp.zeros((96, 128), F32)], axis=0).T
    mom_ref[...] = upright[pairs : pairs + ATOM_DEV, 0:comps]
    for b in range(batches):
        gathered = jnp.zeros((comps, points), F32)
        for i in range(near):
            q = i * batches + b
            gathered = gathered + radial[b, i] * moment[0:comps, q : q + 1]
        value = jnp.sum(gathered, axis=0, keepdims=True)
        pot_ref[b] = jnp.where(wide < sizes_ref[0, b], value, 0.0)
    for copy in started:
        copy.wait_send()


def per_device(
    basis_values,
    density_rows,
    block_mask,
    window_start,
    batch_offsets,
    batch_sizes,
    atom_near,
    harmonics,
    partition,
    radius,
    radial_table,
):
    devs = lax.axis_size("dev")
    ny = devs // NX
    slots, band, size, _ = density_rows.shape
    batches, near = atom_near.shape
    comps, knots = radial_table.shape
    points = basis_values.shape[2]
    dma = pltpu.SemaphoreType.DMA
    vm = pl.BlockSpec(memory_space=pltpu.VMEM)
    sm = pl.BlockSpec(memory_space=pltpu.SMEM)
    hb = pl.BlockSpec(memory_space=pl.ANY)
    block = (band, size, size)
    kept = (band, slots, size, size)
    hops = len(HOPS)
    density, moments, potential = pl.pallas_call(
        functools.partial(kernel, ny),
        name="whole_step",
        out_shape=(
            jax.ShapeDtypeStruct((batches, 1, points), F32),
            jax.ShapeDtypeStruct((ATOM_DEV, comps), F32),
            jax.ShapeDtypeStruct((batches, 1, points), F32),
        ),
        in_specs=[vm, sm, sm, sm, sm, vm, vm, vm, vm, hb, hb],
        out_specs=(vm, vm, vm),
        scratch_shapes=[
            pltpu.VMEM(kept, BF),
            pltpu.VMEM((ny - 1,) + kept, BF),
            pltpu.VMEM((ny,) + block, BF),
            pltpu.VMEM((ny,) + block, BF),
            pltpu.VMEM((ny,) + block, BF),
            pltpu.VMEM((ny,) + block, BF),
            pltpu.VMEM((devs,) + block, BF),
            pltpu.VMEM((8, 128), jnp.int32),
            pltpu.VMEM((ny, NX, 4, 128), jnp.int32),
            pltpu.VMEM((hops, 4, 128), jnp.int32),
            pltpu.VMEM(basis_values.shape, BF),
            pltpu.VMEM(harmonics.shape, BF),
            pltpu.VMEM((batches, band * size, points), BF),
            pltpu.VMEM((batches, near, comps, points), F32),
            pltpu.VMEM((batches, near, comps, points), F32),
            pltpu.VMEM((16, 128), F32),
            pltpu.VMEM((ny, NX, 16, 128), F32),
            pltpu.VMEM((devs, 128 * (1 + hops), 128), BF),
            pltpu.VMEM((64, 128 * (1 + hops)), F32),
            pltpu.VMEM((hops, 32, 128), F32),
            pltpu.VMEM((hops, 32, 128), F32),
            dma((ny - 1, CHUNKS)),
            dma((ny - 1, CHUNKS)),
            dma((ny + 3,)),
            dma((ny + 3,)),
            dma((hops,)),
            dma((hops,)),
            dma((ny, CHUNKS)),
            dma((ny, CHUNKS)),
            dma((ny, CHUNKS)),
            dma((ny, CHUNKS)),
            dma((ny, CHUNKS)),
            dma((ny, CHUNKS)),
            dma((ny, CHUNKS)),
            dma((ny, CHUNKS)),
            dma((ny - 1,)),
            dma((ny - 1,)),
            dma((ny, NX - 1)),
            dma((ny, NX - 1)),
            dma((hops,)),
            dma((hops,)),
            dma((2,)),
        ],
        compiler_params=pltpu.CompilerParams(collective_id=0, has_side_effects=True),
    )(
        density_rows,
        block_mask,
        window_start,
        batch_offsets,
        batch_sizes,
        atom_near.T,
        partition,
        radius,
        radial_table.T,
        basis_values,
        harmonics,
    )
    return density.reshape(batches, points), moments.T, potential.reshape(batches, points)


def solution(mesh):
    placed = (
        P(("region", "dev"), None, None, None),
        P(("region", "dev"), None, None, None),
        P(("region", "dev"), None),
        P(("region", "dev")),
        P(("region", "dev"), None),
        P(("region", "dev"), None),
        P(("region", "dev"), None),
        P(("region", "dev"), None, None, None),
        P(("region", "dev"), None, None),
        P(("region", "dev"), None, None),
        P(),
    )
    return jax.shard_map(
        per_device,
        mesh=mesh,
        in_specs=placed,
        out_specs=(
            P(("region", "dev"), None),
            P(None, ("region", "dev")),
            P(("region", "dev"), None),
        ),
        check_vma=False,
    )
```

```python
import functools

import jax
import jax.numpy as jnp
from jax import lax
from jax.experimental import pallas as pl
from jax.experimental.pallas import tpu as pltpu
from jax.sharding import PartitionSpec as P

ATOM_DEV = 16
NX = 4
CHUNKS = 2
HOPS = (1, 2, -1, -2)
MESH = pl.DeviceIdType.MESH
NT = (((1,), (1,)), ((), ()))
TN = (((0,), (0,)), ((), ()))
F32, BF = jnp.float32, jnp.bfloat16


def remote(src, dst, send_sem, recv_sem, where):
    return pltpu.make_async_remote_copy(
        src_ref=src,
        dst_ref=dst,
        send_sem=send_sem,
        recv_sem=recv_sem,
        device_id=where,
        device_id_type=MESH,
    )


def spline_values(radii, knots):
    knot = lax.broadcasted_iota(jnp.int32, (knots, radii.shape[1]), 0).astype(F32)
    distance = jnp.abs(radii - knot)
    inner = 2.0 / 3.0 - distance * distance + 0.5 * distance * distance * distance
    rest = 2.0 - distance
    outer = rest * rest * rest * (1.0 / 6.0)
    return jnp.where(distance < 1.0, inner, jnp.where(distance < 2.0, outer, 0.0))


def pack(terms, pairs):
    lane = lax.broadcasted_iota(jnp.int32, (8, 128), 1)
    row = lax.broadcasted_iota(jnp.int32, (8, 128), 0)
    third = terms[16:24]
    last = jnp.broadcast_to(terms[24:25], (8, 128))
    top = jnp.where(lane < pairs, terms[0:8], pltpu.roll(third, 72, 1))
    tail = jnp.where(row == 0, pltpu.roll(last, 88, 1), jnp.where(row == 1, pltpu.roll(last, 48, 1), 0.0))
    low = jnp.where(lane < pairs, terms[8:16], jnp.where(lane < 88, pltpu.roll(third, 16, 1), tail))
    return top, low


def unpack(top, low, pairs):
    lane = lax.broadcasted_iota(jnp.int32, (8, 128), 1)
    row = lax.broadcasted_iota(jnp.int32, (8, 128), 0)
    live = lane < pairs
    first = jnp.where(live, top, 0.0)
    second = jnp.where(live, low, 0.0)
    third = jnp.where(lane < 56, pltpu.roll(top, 56, 1), jnp.where(live, pltpu.roll(low, 112, 1), 0.0))
    zero = jnp.broadcast_to(low[0:1], (8, 128))
    one = jnp.broadcast_to(low[1:2], (8, 128))
    last = jnp.where(lane < 40, pltpu.roll(zero, 40, 1), jnp.where(live, pltpu.roll(one, 80, 1), 0.0))
    last = jnp.where(row == 0, last, 0.0)
    return jnp.concatenate([first, second, third, last], axis=0)


def kernel(
    ny,
    rows_ref,
    mask_ref,
    start_ref,
    offsets_ref,
    sizes_ref,
    near_ref,
    part_ref,
    radius_ref,
    radial_ref,
    basis_hbm,
    harm_hbm,
    dens_ref,
    mom_ref,
    pot_ref,
    own,
    hold,
    out_r,
    out_l,
    out_o,
    relay,
    swap,
    across,
    win,
    line,
    metas,
    asked,
    basis,
    harm,
    turned,
    parted,
    radial,
    packed,
    every,
    hot,
    sums,
    answer,
    got,
    ys,
    yr,
    ms,
    mr,
    qs,
    qr,
    rs,
    ls,
    os_,
    fr,
    fl,
    fo,
    frel,
    fws,
    sws,
    swr,
    acs,
    acr,
    ts,
    tr,
    xs,
    xr_,
    zs,
    zr,
    local,
):
    region, me = lax.axis_index("region"), lax.axis_index("dev")
    regions, devs = lax.axis_size("region"), ny * NX
    x, y = me % NX, me // NX
    far = ny // 2
    xr, xl, xo = (x + 1) % NX, (x + NX - 1) % NX, (x + 2) % NX
    right, left, other = ({"dev": y * NX + xx} for xx in (xr, xl, xo))
    ups = [{"dev": ((y + s) % ny) * NX + x} for s in range(1, ny)]
    up, down = ups[0], ups[-1]
    nears = [{"region": (region + h + regions) % regions} for h in HOPS]
    slots, band, size, _ = rows_ref.shape
    step = band // CHUNKS
    near, batches = near_ref.shape
    pairs = near * batches
    knots, comps = radial_ref.shape
    points = part_ref.shape[2]
    started = []

    def go(copy):
        copy.start()
        started.append(copy)

    barrier = pltpu.get_barrier_semaphore()
    greeted = ups + [right, left, other] + nears
    for peer in greeted:
        pl.semaphore_signal(barrier, inc=1, device_id=peer, device_id_type=MESH)
    fetch_basis = pltpu.make_async_copy(basis_hbm, basis, local.at[0])
    fetch_basis.start()
    fetch_harm = pltpu.make_async_copy(harm_hbm, harm, local.at[1])
    fetch_harm.start()

    for t in range(slots):
        for k in range(band):
            keep = jnp.full((1, 1), mask_ref[t, k], jnp.int32).astype(F32).astype(BF)
            own[k, t] = rows_ref[t, k] * keep

    lane = lax.broadcasted_iota(jnp.int32, (1, 128), 1)
    line[...] = jnp.zeros_like(line)
    line[0:near, 0:batches] = near_ref[...]
    total = jnp.zeros((1, 128), jnp.int32)
    for i in range(near):
        moved = pltpu.roll(jnp.broadcast_to(line[i : i + 1, :], (8, 128)), i * batches, 1)[0:1]
        total = jnp.where((lane >= i * batches) & (lane < (i + 1) * batches), moved, total)
    atom_region = ATOM_DEV * devs
    bits = atom_region.bit_length() - 1
    side = region + lax.shift_right_logical(total, bits) - 1
    side = jnp.where(side < 0, side + regions, jnp.where(side >= regions, side - regions, side))
    target = side * atom_region + (total & (atom_region - 1))
    owned = region * atom_region + me * ATOM_DEV + lane - pairs
    whole_line = jnp.where(lane < pairs, target, jnp.where(lane < pairs + ATOM_DEV, owned, -1))
    start = start_ref[0]
    line[0:1] = whole_line
    line[1:2] = jnp.full((1, 128), start // devs, jnp.int32)
    line[2:3] = jnp.full((1, 128), start % devs, jnp.int32)
    metas[0, x] = line[0:4]
    pl.semaphore_wait(barrier, len(greeted))

    def part_of(ref, c):
        return ref.at[pl.ds(c * step, step)]

    for c in range(CHUNKS):
        go(remote(part_of(own, c), part_of(hold.at[0], c), ys.at[0, c], yr.at[0, c], down))
        go(remote(part_of(own, c), part_of(hold.at[far], c), ys.at[far, c], yr.at[far, c], up))
        if c == 0:
            for i, peer in enumerate((right, left, other)):
                go(remote(line.at[0:4], metas.at[0, x], ms.at[i], mr.at[i], peer))
    for i in range(len(HOPS)):
        go(remote(line.at[0:4], asked.at[i], qs.at[i], qr.at[i], nears[i]))

    for i, xx in enumerate((xl, xr, xo)):
        remote(line.at[0:4], metas.at[0, xx], ms.at[i], mr.at[i], right).wait_recv()
    lone, halfway = band - 1, size // 2
    first_half, second_half = pl.ds(0, halfway), pl.ds(halfway, halfway)
    go(remote(own.at[lone, :, first_half], swap.at[0], sws.at[0], swr.at[0], right))
    go(remote(own.at[lone, :, second_half], swap.at[1], sws.at[1], swr.at[1], left))
    base = 3
    go(remote(metas.at[0], metas.at[1], ms.at[base], mr.at[base], down))
    go(remote(metas.at[0], metas.at[ny - 1], ms.at[base + far], mr.at[base + far], up))

    order = [0]
    for s in range(1, far + 1):
        order.append(s)
        if s < far:
            order.append(-s)

    def row_of(g):
        return (y + order[g] + ny) % ny

    def weights(xx, d):
        q = metas[0, xx, 1:2, :]
        m = metas[0, xx, 2:3, :]
        slot = q + jnp.where(m > d, 1, 0)
        slot = jnp.where(slot >= slots, slot - slots, slot)
        return [jnp.where(slot == t, 1.0, 0.0).astype(F32).astype(BF) for t in range(slots)]

    def other_part(c):
        low, high = c * step, min((c + 1) * step, lone)
        return pl.ds(low, high - low) if high > low else None

    def via_right(g, c):
        return (g + c) % 2 == 0

    def process(g, c):
        rho = order[g]
        d = row_of(g) * NX + x
        source = own if rho == 0 else hold.at[rho - 1 if rho > 0 else far - rho - 1]
        picks = [(dst, weights(xx, d)) for xx, dst in ((xr, out_r.at[g]), (xl, out_l.at[g]), (xo, out_o.at[g]), (x, win.at[d]))]
        for k in range(c * step, (c + 1) * step):
            parts = [source[k, t] for t in range(slots)]
            for n, (dst, w) in enumerate(picks):
                if n == 2 and k == lone:
                    continue
                chosen = parts[0] * w[0]
                for t in range(1, slots):
                    chosen = chosen + parts[t] * w[t]
                dst[k] = chosen
        if other_part(c) is not None:
            some = other_part(c)
            go(remote(out_o.at[g, some], relay.at[g, some], os_.at[g, c], frel.at[g, c], right if via_right(g, c) else left))
        go(remote(part_of(out_r.at[g], c), part_of(win.at[d], c), rs.at[g, c], fl.at[g, c], right))
        go(remote(part_of(out_l.at[g], c), part_of(win.at[d], c), ls.at[g, c], fr.at[g, c], left))

    def passing(g, c):
        some = other_part(c)
        if some is None:
            return
        toward, origin = (right, xl) if via_right(g, c) else (left, xr)
        d = row_of(g) * NX + origin
        remote(out_o.at[g, some], relay.at[g, some], os_.at[g, c], frel.at[g, c], right).wait_recv()
        go(remote(relay.at[g, some], win.at[d, some], fws.at[g, c], fo.at[g, c], toward))

    def take(g):
        rho = order[g]
        d = row_of(g) * NX + xo
        source = across.at[0 if rho == 0 else (rho if rho > 0 else far - rho)]
        w = weights(x, d)
        chosen = source[0] * w[0]
        for t in range(1, slots):
            chosen = chosen + source[t] * w[t]
        win[d, lone] = chosen

    def across_in(s):
        i, j = s - 1, far + s - 1
        remote(across.at[0], across.at[1 + i], acs.at[i], acr.at[i], down).wait_recv()
        if s < far:
            go(remote(across.at[1 + i], across.at[2 + i], acs.at[i + 1], acr.at[i + 1], down))
            remote(across.at[0], across.at[1 + j], acs.at[j], acr.at[j], up).wait_recv()
            if s < far - 1:
                go(remote(across.at[1 + j], across.at[2 + j], acs.at[j + 1], acr.at[j + 1], up))
        take(2 * s - 1)
        if s < far:
            take(2 * s)

    def prepare(b, carry):
        for j in range(band):
            turned[b, j * size : (j + 1) * size, :] = basis[b, j].T
        for i in range(near):
            values = harm[b, i].astype(F32)
            parted[b, i] = values * part_ref[b, i : i + 1, :]
            spline = spline_values(radius_ref[b, i : i + 1, :], knots)
            curve = lax.dot_general(
                radial_ref[...], spline, TN, precision=lax.Precision.HIGHEST, preferred_element_type=F32
            )
            radial[b, i] = values * curve
        return carry

    def fill(slot, asked_line):
        column = jnp.broadcast_to(asked_line, (128, 128)).T

        def one(t, carry):
            r = lax.rem(t // NX + ny - y, ny)
            wanted = metas[r, t % NX, 0:1, :]
            same = jnp.where(column == wanted, 1.0, 0.0).astype(F32)
            hot[t, slot * 128 : (slot + 1) * 128, :] = same.astype(BF)
            return carry

        lax.fori_loop(0, devs, one, 0)

    for c in range(CHUNKS):
        process(0, c)
    remote(own.at[lone, :, first_half], swap.at[0], sws.at[0], swr.at[0], right).wait_recv()
    go(remote(swap.at[0], across.at[0, :, first_half], sws.at[2], swr.at[2], right))
    remote(own.at[lone, :, second_half], swap.at[1], sws.at[1], swr.at[1], left).wait_recv()
    go(remote(swap.at[1], across.at[0, :, second_half], sws.at[3], swr.at[3], left))
    fetch_basis.wait()
    fetch_harm.wait()
    per = -(-batches // (CHUNKS * (far - 1)))
    ready = 0
    lag = []
    for s in range(1, far + 1):
        i, j = s - 1, far + s - 1
        for c in range(CHUNKS):
            remote(part_of(own, c), part_of(hold.at[i], c), ys.at[i, c], yr.at[i, c], down).wait_recv()
            if s < far - 1 or (s < far and c % 2 == 0):
                go(remote(part_of(hold.at[i], c), part_of(hold.at[i + 1], c), ys.at[i + 1, c], yr.at[i + 1, c], down))
            if s < far:
                remote(part_of(own, c), part_of(hold.at[j], c), ys.at[j, c], yr.at[j, c], up).wait_recv()
                if s < far - 1:
                    go(remote(part_of(hold.at[j], c), part_of(hold.at[j + 1], c), ys.at[j + 1, c], yr.at[j + 1, c], up))
                elif c % 2 == 1:
                    go(remote(part_of(hold.at[j], c), part_of(hold.at[far - 1], c), ys.at[far - 1, c], yr.at[far - 1, c], up))
            if c == 0:
                remote(metas.at[0], metas.at[s], ms.at[base + i], mr.at[base + i], down).wait_recv()
                if s < far:
                    go(remote(metas.at[s], metas.at[s + 1], ms.at[base + i + 1], mr.at[base + i + 1], down))
                    remote(metas.at[0], metas.at[ny - s], ms.at[base + j], mr.at[base + j], up).wait_recv()
                    if s < far - 1:
                        go(remote(metas.at[ny - s], metas.at[ny - s - 1], ms.at[base + j + 1], mr.at[base + j + 1], up))
            process(2 * s - 1, c)
            if s < far:
                process(2 * s, c)
            if s == 1:
                lag.append((0, c))
            else:
                lag.append((2 * s - 3, c))
                lag.append((2 * s - 2, c))
            while lag:
                passing(*lag.pop(0))
            if ready < batches and s < far:
                upto = min(batches, ready + per)
                lax.fori_loop(ready, upto, prepare, 0)
                ready = upto
        if s == 1:
            remote(swap.at[0], across.at[0, :, first_half], sws.at[2], swr.at[2], right).wait_recv()
            remote(swap.at[1], across.at[0, :, second_half], sws.at[3], swr.at[3], left).wait_recv()
            go(remote(across.at[0], across.at[1], acs.at[0], acr.at[0], down))
            go(remote(across.at[0], across.at[1 + far], acs.at[far], acr.at[far], up))
            take(0)
        else:
            across_in(s - 1)
    for i in range(len(HOPS)):
        remote(line.at[0:4], asked.at[i], qs.at[i], qr.at[i], nears[0]).wait_recv()
    fill(0, metas[0, x, 0:1, :])
    fill(1, asked[0, 0:1, :])
    for c in range(CHUNKS):
        passing(ny - 1, c)
    for i in range(1, len(HOPS)):
        fill(1 + i, asked[i, 0:1, :])
    across_in(far)
    for g in range(ny):
        row = row_of(g) * NX
        for c in range(CHUNKS):
            remote(part_of(out_r.at[g], c), part_of(win.at[row + xl], c), rs.at[g, c], fl.at[g, c], right).wait_recv()
            remote(part_of(out_l.at[g], c), part_of(win.at[row + xr], c), ls.at[g, c], fr.at[g, c], left).wait_recv()
            some = other_part(c)
            if some is not None:
                remote(out_o.at[g, some], win.at[row + xo, some], fws.at[g, c], fo.at[g, c], right).wait_recv()

    zero = jnp.zeros((size, size), BF)
    wide = lax.broadcasted_iota(jnp.int32, (1, points), 1)
    spot = lax.broadcasted_iota(jnp.int32, (comps, 128), 1)

    def batch(b, gained):
        first = start + offsets_ref[0, b]
        places = [lax.rem(first + j, devs) for j in range(band)]

        def piece(j, k):
            return win[places[j], k]

        def quad(a, b_, c, d):
            return jnp.concatenate([jnp.concatenate([a, b_], axis=1), jnp.concatenate([c, d], axis=1)], axis=0)

        low, high = turned[b, 0 : 2 * size, :], turned[b, 2 * size : 4 * size, :]
        dot = functools.partial(jnp.dot, preferred_element_type=F32)
        m01 = dot(quad(piece(0, 1), piece(0, 2), piece(1, 0), piece(1, 1)), low)
        m01 = m01 + dot(quad(piece(0, 3), zero, piece(1, 2), piece(1, 3)), high)
        m23 = dot(quad(piece(2, 1), piece(2, 2), piece(3, 0), piece(3, 1)), high)
        m2x = dot(piece(2, 0), turned[b, size : 2 * size, :])
        density = jnp.sum(m01 * low.astype(F32) + m23 * high.astype(F32), axis=0, keepdims=True)
        density = density + jnp.sum(m2x * turned[b, 2 * size : 3 * size, :].astype(F32), axis=0, keepdims=True)
        density = jnp.where(wide < sizes_ref[0, b], density, 0.0)
        dens_ref[pl.ds(b, 1), :] = density
        for i in range(near):
            column = jnp.sum(parted[b, i] * density, axis=1, keepdims=True)
            gained = jnp.where(spot == i * batches + b, column, gained)
        return gained

    terms = lax.fori_loop(0, batches, batch, jnp.zeros((comps, 128), F32), unroll=4)
    top, low = pack(terms, pairs)
    packed[0:8] = top
    packed[8:16] = low

    sides = [{"dev": y * NX + (x + s) % NX} for s in range(1, NX)]
    for i in range(ny - 1):
        go(remote(packed, every.at[y, x], ts.at[i], tr.at[i], ups[i]))
    for i in range(NX - 1):
        go(remote(packed, every.at[y, x], xs.at[0, i], xr_.at[0, i], sides[i]))
    every[y, x] = packed[...]
    near_first = sorted(range(1, ny), key=lambda j: min(j, ny - j))

    def spread(j):
        yy = (y + ny - j) % ny
        remote(packed, every.at[yy, x], ts.at[j - 1], tr.at[j - 1], up).wait_recv()
        for i in range(NX - 1):
            go(remote(every.at[yy, x], every.at[yy, x], xs.at[j, i], xr_.at[j, i], sides[i]))

    sums[...] = jnp.zeros_like(sums)

    def collect(j):
        yy = (y + ny - j) % ny
        for i in range(NX - 1):
            xx = (x + NX - 1 - i) % NX
            remote(packed, every.at[yy, xx], xs.at[j, i], xr_.at[j, i], right).wait_recv()
        for pair in range(NX // 2):
            lefts, rights = [], []
            for xx in (2 * pair, 2 * pair + 1):
                value = unpack(every[yy, xx, 0:8], every[yy, xx, 8:16], pairs)
                high = value.astype(BF)
                lowp = (value - high.astype(F32)).astype(BF)
                lefts.append(jnp.concatenate([high, lowp], axis=0))
                rights.append(hot[yy * NX + xx])
            sums[...] += lax.dot_general(
                jnp.concatenate(lefts, axis=1), jnp.concatenate(rights, axis=1), NT, preferred_element_type=F32
            )

    for j in near_first:
        spread(j)
    collect(0)
    for j in near_first:
        collect(j)
    both = sums[0:32, :] + sums[32:64, :]
    for i in range(len(HOPS)):
        answer[i] = both[:, 128 * (i + 1) : 128 * (i + 2)]
    for i in range(len(HOPS)):
        back = {"region": (region - HOPS[i] + regions) % regions}
        go(remote(answer.at[i], got.at[i], zs.at[i], zr.at[i], back))
    moment = both[:, 0:128]
    for i in range(len(HOPS)):
        remote(answer.at[i], got.at[i], zs.at[i], zr.at[i], nears[0]).wait_recv()
        moment = moment + got[i]
    upright = jnp.concatenate([moment, jnp.zeros((96, 128), F32)], axis=0).T
    mom_ref[...] = upright[pairs : pairs + ATOM_DEV, 0:comps]
    for b in range(batches):
        gathered = jnp.zeros((comps, points), F32)
        for i in range(near):
            q = i * batches + b
            gathered = gathered + radial[b, i] * moment[0:comps, q : q + 1]
        value = jnp.sum(gathered, axis=0, keepdims=True)
        pot_ref[b : b + 1, :] = jnp.where(wide < sizes_ref[0, b], value, 0.0)
    for copy in started:
        copy.wait_send()


def hand_over(*arrays):
    def copies(*refs):
        for source, target in zip(refs[: len(arrays)], refs[len(arrays) :]):
            target[...] = source[...]

    vm = pl.BlockSpec(memory_space=pltpu.VMEM)
    return pl.pallas_call(
        copies,
        name="hand_over",
        out_shape=tuple(jax.ShapeDtypeStruct(a.shape, a.dtype) for a in arrays),
        in_specs=[vm] * len(arrays),
        out_specs=(vm,) * len(arrays),
    )(*arrays)


def per_device(
    basis_values,
    density_rows,
    block_mask,
    window_start,
    batch_offsets,
    batch_sizes,
    atom_near,
    harmonics,
    partition,
    radius,
    radial_table,
):
    devs = lax.axis_size("dev")
    ny = devs // NX
    slots, band, size, _ = density_rows.shape
    batches, near = atom_near.shape
    comps, knots = radial_table.shape
    points = basis_values.shape[2]
    dma = pltpu.SemaphoreType.DMA
    vm = pl.BlockSpec(memory_space=pltpu.VMEM)
    sm = pl.BlockSpec(memory_space=pltpu.SMEM)
    hb = pl.BlockSpec(memory_space=pl.ANY)
    block = (band, size, size)
    kept = (band, slots, size, size)
    hops = len(HOPS)
    density, moments, potential = pl.pallas_call(
        functools.partial(kernel, ny),
        name="whole_step",
        out_shape=(
            jax.ShapeDtypeStruct((batches, points), F32),
            jax.ShapeDtypeStruct((ATOM_DEV, comps), F32),
            jax.ShapeDtypeStruct((batches, points), F32),
        ),
        in_specs=[vm, sm, sm, sm, sm, vm, vm, vm, vm, hb, hb],
        out_specs=(vm, vm, vm),
        scratch_shapes=[
            pltpu.VMEM(kept, BF),
            pltpu.VMEM((ny - 1,) + kept, BF),
            pltpu.VMEM((ny,) + block, BF),
            pltpu.VMEM((ny,) + block, BF),
            pltpu.VMEM((ny,) + block, BF),
            pltpu.VMEM((ny,) + block, BF),
            pltpu.VMEM((2, slots, size // 2, size), BF),
            pltpu.VMEM((ny, slots, size, size), BF),
            pltpu.VMEM((devs,) + block, BF),
            pltpu.VMEM((8, 128), jnp.int32),
            pltpu.VMEM((ny, NX, 4, 128), jnp.int32),
            pltpu.VMEM((hops, 4, 128), jnp.int32),
            pltpu.VMEM(basis_values.shape, BF),
            pltpu.VMEM(harmonics.shape, BF),
            pltpu.VMEM((batches, band * size, points), BF),
            pltpu.VMEM((batches, near, comps, points), F32),
            pltpu.VMEM((batches, near, comps, points), F32),
            pltpu.VMEM((16, 128), F32),
            pltpu.VMEM((ny, NX, 16, 128), F32),
            pltpu.VMEM((devs, 128 * (1 + hops), 128), BF),
            pltpu.VMEM((64, 128 * (1 + hops)), F32),
            pltpu.VMEM((hops, 32, 128), F32),
            pltpu.VMEM((hops, 32, 128), F32),
            dma((ny - 1, CHUNKS)),
            dma((ny - 1, CHUNKS)),
            dma((ny + 3,)),
            dma((ny + 3,)),
            dma((hops,)),
            dma((hops,)),
            dma((ny, CHUNKS)),
            dma((ny, CHUNKS)),
            dma((ny, CHUNKS)),
            dma((ny, CHUNKS)),
            dma((ny, CHUNKS)),
            dma((ny, CHUNKS)),
            dma((ny, CHUNKS)),
            dma((ny, CHUNKS)),
            dma((4,)),
            dma((4,)),
            dma((ny - 1,)),
            dma((ny - 1,)),
            dma((ny - 1,)),
            dma((ny - 1,)),
            dma((ny, NX - 1)),
            dma((ny, NX - 1)),
            dma((hops,)),
            dma((hops,)),
            dma((2,)),
        ],
        compiler_params=pltpu.CompilerParams(collective_id=0, has_side_effects=True),
    )(
        density_rows,
        block_mask,
        window_start,
        batch_offsets,
        batch_sizes,
        atom_near.T,
        partition,
        radius,
        radial_table.T,
        basis_values,
        harmonics,
    )
    density, moments, potential = hand_over(density, moments, potential)
    return density, moments.T, potential


def solution(mesh):
    placed = (
        P(("region", "dev"), None, None, None),
        P(("region", "dev"), None, None, None),
        P(("region", "dev"), None),
        P(("region", "dev")),
        P(("region", "dev"), None),
        P(("region", "dev"), None),
        P(("region", "dev"), None),
        P(("region", "dev"), None, None, None),
        P(("region", "dev"), None, None),
        P(("region", "dev"), None, None),
        P(),
    )
    return jax.shard_map(
        per_device,
        mesh=mesh,
        in_specs=placed,
        out_specs=(
            P(("region", "dev"), None),
            P(None, ("region", "dev")),
            P(("region", "dev"), None),
        ),
        check_vma=False,
    )
```

```python
import functools

import jax
import jax.numpy as jnp
from jax import lax
from jax.experimental import pallas as pl
from jax.experimental.pallas import tpu as pltpu
from jax.sharding import PartitionSpec as P

ATOM_DEV = 16
NX = 4
CHUNKS = 2
HOPS = (1, 2, -1, -2)
MESH = pl.DeviceIdType.MESH
NT = (((1,), (1,)), ((), ()))
TN = (((0,), (0,)), ((), ()))
F32, BF = jnp.float32, jnp.bfloat16


def remote(src, dst, send_sem, recv_sem, where):
    return pltpu.make_async_remote_copy(
        src_ref=src,
        dst_ref=dst,
        send_sem=send_sem,
        recv_sem=recv_sem,
        device_id=where,
        device_id_type=MESH,
    )


def spline_values(radii, knots):
    knot = lax.broadcasted_iota(jnp.int32, (knots, radii.shape[1]), 0).astype(F32)
    distance = jnp.abs(radii - knot)
    inner = 2.0 / 3.0 - distance * distance + 0.5 * distance * distance * distance
    rest = 2.0 - distance
    outer = rest * rest * rest * (1.0 / 6.0)
    return jnp.where(distance < 1.0, inner, jnp.where(distance < 2.0, outer, 0.0))


def pack(terms, pairs):
    lane = lax.broadcasted_iota(jnp.int32, (8, 128), 1)
    row = lax.broadcasted_iota(jnp.int32, (8, 128), 0)
    third = terms[16:24]
    last = jnp.broadcast_to(terms[24:25], (8, 128))
    top = jnp.where(lane < pairs, terms[0:8], pltpu.roll(third, 72, 1))
    tail = jnp.where(row == 0, pltpu.roll(last, 88, 1), jnp.where(row == 1, pltpu.roll(last, 48, 1), 0.0))
    low = jnp.where(lane < pairs, terms[8:16], jnp.where(lane < 88, pltpu.roll(third, 16, 1), tail))
    return top, low


def unpack(top, low, pairs):
    lane = lax.broadcasted_iota(jnp.int32, (8, 128), 1)
    row = lax.broadcasted_iota(jnp.int32, (8, 128), 0)
    live = lane < pairs
    first = jnp.where(live, top, 0.0)
    second = jnp.where(live, low, 0.0)
    third = jnp.where(lane < 56, pltpu.roll(top, 56, 1), jnp.where(live, pltpu.roll(low, 112, 1), 0.0))
    zero = jnp.broadcast_to(low[0:1], (8, 128))
    one = jnp.broadcast_to(low[1:2], (8, 128))
    last = jnp.where(lane < 40, pltpu.roll(zero, 40, 1), jnp.where(live, pltpu.roll(one, 80, 1), 0.0))
    last = jnp.where(row == 0, last, 0.0)
    return jnp.concatenate([first, second, third, last], axis=0)


def kernel(
    ny,
    rows_hbm,
    mask_ref,
    start_ref,
    offsets_ref,
    sizes_ref,
    near_ref,
    part_hbm,
    radius_hbm,
    radial_ref,
    basis_hbm,
    harm_hbm,
    dens_ref,
    mom_ref,
    pot_ref,
    rows_ref,
    part_ref,
    radius_ref,
    own,
    hold,
    out_r,
    out_l,
    out_o,
    relay,
    swap,
    across,
    win,
    line,
    metas,
    asked,
    basis,
    harm,
    turned,
    parted,
    radial,
    packed,
    every,
    hot,
    sums,
    answer,
    got,
    ys,
    yr,
    ms,
    mr,
    qs,
    qr,
    rs,
    ls,
    os_,
    fr,
    fl,
    fo,
    frel,
    fws,
    sws,
    swr,
    acs,
    acr,
    ts,
    tr,
    xs,
    xr_,
    zs,
    zr,
    local,
):
    region, me = lax.axis_index("region"), lax.axis_index("dev")
    regions, devs = lax.axis_size("region"), ny * NX
    x, y = me % NX, me // NX
    far = ny // 2
    xr, xl, xo = (x + 1) % NX, (x + NX - 1) % NX, (x + 2) % NX
    right, left, other = ({"dev": y * NX + xx} for xx in (xr, xl, xo))
    ups = [{"dev": ((y + s) % ny) * NX + x} for s in range(1, ny)]
    up, down = ups[0], ups[-1]
    nears = [{"region": (region + h + regions) % regions} for h in HOPS]
    slots, band, size, _ = rows_ref.shape
    step = band // CHUNKS
    near, batches = near_ref.shape
    pairs = near * batches
    knots, comps = radial_ref.shape
    points = part_ref.shape[2]
    started = []

    def go(copy):
        copy.start()
        started.append(copy)

    barrier = pltpu.get_barrier_semaphore()
    greeted = [up, down, right, left, other] + nears
    for peer in greeted:
        pl.semaphore_signal(barrier, inc=1, device_id=peer, device_id_type=MESH)
    fetch_rows = pltpu.make_async_copy(rows_hbm, rows_ref, local.at[2])
    fetch_rows.start()
    fetches = [
        pltpu.make_async_copy(source, target, local.at[n])
        for source, target, n in (
            (basis_hbm, basis, 0),
            (harm_hbm, harm, 1),
            (part_hbm, part_ref, 3),
            (radius_hbm, radius_ref, 4),
        )
    ]

    lane = lax.broadcasted_iota(jnp.int32, (1, 128), 1)
    line[...] = jnp.zeros_like(line)
    line[0:near, 0:batches] = near_ref[...]
    total = jnp.zeros((1, 128), jnp.int32)
    for i in range(near):
        moved = pltpu.roll(jnp.broadcast_to(line[i : i + 1, :], (8, 128)), i * batches, 1)[0:1]
        total = jnp.where((lane >= i * batches) & (lane < (i + 1) * batches), moved, total)
    atom_region = ATOM_DEV * devs
    bits = atom_region.bit_length() - 1
    side = region + lax.shift_right_logical(total, bits) - 1
    side = jnp.where(side < 0, side + regions, jnp.where(side >= regions, side - regions, side))
    target = side * atom_region + (total & (atom_region - 1))
    owned = region * atom_region + me * ATOM_DEV + lane - pairs
    whole_line = jnp.where(lane < pairs, target, jnp.where(lane < pairs + ATOM_DEV, owned, -1))
    start = start_ref[0]
    line[0:1] = whole_line
    line[1:2] = jnp.full((1, 128), start // devs, jnp.int32)
    line[2:3] = jnp.full((1, 128), start % devs, jnp.int32)
    metas[0, x] = line[0:4]
    fetch_rows.wait()
    for t in range(slots):
        for k in range(band):
            keep = jnp.full((1, 1), mask_ref[t, k], jnp.int32).astype(F32).astype(BF)
            own[k, t] = rows_ref[t, k] * keep
    pl.semaphore_wait(barrier, len(greeted))

    def part_of(ref, c):
        return ref.at[pl.ds(c * step, step)]

    for c in range(CHUNKS):
        go(remote(part_of(own, c), part_of(hold.at[0], c), ys.at[0, c], yr.at[0, c], down))
        go(remote(part_of(own, c), part_of(hold.at[far], c), ys.at[far, c], yr.at[far, c], up))
        if c == 0:
            for i, peer in enumerate((right, left, other)):
                go(remote(line.at[0:4], metas.at[0, x], ms.at[i], mr.at[i], peer))
    for i in range(len(HOPS)):
        go(remote(line.at[0:4], asked.at[i], qs.at[i], qr.at[i], nears[i]))

    for copy in fetches:
        copy.start()

    def row_meta(i):
        remote(line.at[0:4], metas.at[0, (xl, xr, xo)[i]], ms.at[i], mr.at[i], right).wait_recv()

    row_meta(0)
    row_meta(1)
    lone, halfway = band - 1, size // 2
    first_half, second_half = pl.ds(0, halfway), pl.ds(halfway, halfway)
    go(remote(own.at[lone, :, first_half], swap.at[0], sws.at[0], swr.at[0], right))
    go(remote(own.at[lone, :, second_half], swap.at[1], sws.at[1], swr.at[1], left))
    base = 3

    order = [0]
    for s in range(1, far + 1):
        order.append(s)
        if s < far:
            order.append(-s)

    def row_of(g):
        return (y + order[g] + ny) % ny

    def weights(xx, d):
        q = metas[0, xx, 1:2, :]
        m = metas[0, xx, 2:3, :]
        slot = q + jnp.where(m > d, 1, 0)
        slot = jnp.where(slot >= slots, slot - slots, slot)
        return [jnp.where(slot == t, 1.0, 0.0).astype(F32).astype(BF) for t in range(slots)]

    def other_part(c):
        low, high = c * step, min((c + 1) * step, lone)
        return pl.ds(low, high - low) if high > low else None

    def straight(g, c):
        return g == ny - 1 and c == CHUNKS - 1

    def via_right(g, c):
        return (g + c) % 2 == 0

    def process(g, c, some=(0, 1, 2, 3)):
        rho = order[g]
        d = row_of(g) * NX + x
        source = own if rho == 0 else hold.at[rho - 1 if rho > 0 else far - rho - 1]
        picks = ((xr, out_r.at[g]), (xl, out_l.at[g]), (xo, out_o.at[g]), (x, win.at[d]))
        picks = [(n, (picks[n][1], weights(picks[n][0], d))) for n in some]
        for k in range(c * step, (c + 1) * step):
            parts = [source[k, t] for t in range(slots)]
            for n, (dst, w) in picks:
                if n == 2 and k == lone:
                    continue
                chosen = parts[0] * w[0]
                for t in range(1, slots):
                    chosen = chosen + parts[t] * w[t]
                dst[k] = chosen
        if 2 in some and other_part(c) is not None:
            piece = other_part(c)
            if straight(g, c):
                go(remote(out_o.at[g, piece], win.at[d, piece], os_.at[g, c], fo.at[g, c], other))
            else:
                go(remote(out_o.at[g, piece], relay.at[g, piece], os_.at[g, c], frel.at[g, c], right if via_right(g, c) else left))
        if 0 not in some:
            return
        go(remote(part_of(out_r.at[g], c), part_of(win.at[d], c), rs.at[g, c], fl.at[g, c], right))
        go(remote(part_of(out_l.at[g], c), part_of(win.at[d], c), ls.at[g, c], fr.at[g, c], left))

    def passing(g, c):
        some = other_part(c)
        if some is None or straight(g, c):
            return
        toward, origin = (right, xl) if via_right(g, c) else (left, xr)
        d = row_of(g) * NX + origin
        remote(out_o.at[g, some], relay.at[g, some], os_.at[g, c], frel.at[g, c], right).wait_recv()
        go(remote(relay.at[g, some], win.at[d, some], fws.at[g, c], fo.at[g, c], toward))

    def take(g):
        rho = order[g]
        d = row_of(g) * NX + xo
        source = across.at[0 if rho == 0 else (rho if rho > 0 else far - rho)]
        w = weights(x, d)
        chosen = source[0] * w[0]
        for t in range(1, slots):
            chosen = chosen + source[t] * w[t]
        win[d, lone] = chosen

    def across_in(s):
        i, j = s - 1, far + s - 1
        remote(across.at[0], across.at[1 + i], acs.at[i], acr.at[i], down).wait_recv()
        if s < far:
            go(remote(across.at[1 + i], across.at[2 + i], acs.at[i + 1], acr.at[i + 1], down))
            remote(across.at[0], across.at[1 + j], acs.at[j], acr.at[j], up).wait_recv()
            if s < far - 1:
                go(remote(across.at[1 + j], across.at[2 + j], acs.at[j + 1], acr.at[j + 1], up))
        take(2 * s - 1)
        if s < far:
            take(2 * s)

    def prepare(b, carry):
        for j in range(band):
            turned[b, j * size : (j + 1) * size, :] = basis[b, j].T
        for i in range(near):
            values = harm[b, i].astype(F32)
            parted[b, i] = values * part_ref[b, i : i + 1, :]
            spline = spline_values(radius_ref[b, i : i + 1, :], knots)
            curve = lax.dot_general(
                radial_ref[...], spline, TN, precision=lax.Precision.HIGHEST, preferred_element_type=F32
            )
            radial[b, i] = values * curve
        return carry

    def fill(slot, asked_line):
        column = jnp.broadcast_to(asked_line, (128, 128)).T

        def one(t, carry):
            r = lax.rem(t // NX + ny - y, ny)
            wanted = metas[r, t % NX, 0:1, :]
            same = jnp.where(column == wanted, 1.0, 0.0).astype(F32)
            hot[t, slot * 128 : (slot + 1) * 128, :] = same.astype(BF)
            return carry

        lax.fori_loop(0, devs, one, 0)

    for c in range(CHUNKS):
        process(0, c, (0, 1))
    row_meta(2)
    go(remote(metas.at[0], metas.at[1], ms.at[base], mr.at[base], down))
    go(remote(metas.at[0], metas.at[ny - 1], ms.at[base + far], mr.at[base + far], up))
    for c in range(CHUNKS):
        process(0, c, (2, 3))
    remote(own.at[lone, :, first_half], swap.at[0], sws.at[0], swr.at[0], right).wait_recv()
    go(remote(swap.at[0], across.at[0, :, first_half], sws.at[2], swr.at[2], right))
    remote(own.at[lone, :, second_half], swap.at[1], sws.at[1], swr.at[1], left).wait_recv()
    go(remote(swap.at[1], across.at[0, :, second_half], sws.at[3], swr.at[3], left))
    for copy in fetches:
        copy.wait()
    per = -(-batches // (CHUNKS * (far - 1)))
    ready = 0
    lag = []
    for s in range(1, far + 1):
        i, j = s - 1, far + s - 1
        for c in range(CHUNKS):
            remote(part_of(own, c), part_of(hold.at[i], c), ys.at[i, c], yr.at[i, c], down).wait_recv()
            if s < far - 1 or (s < far and c % 2 == 0):
                go(remote(part_of(hold.at[i], c), part_of(hold.at[i + 1], c), ys.at[i + 1, c], yr.at[i + 1, c], down))
            if s < far:
                remote(part_of(own, c), part_of(hold.at[j], c), ys.at[j, c], yr.at[j, c], up).wait_recv()
                if s < far - 1:
                    go(remote(part_of(hold.at[j], c), part_of(hold.at[j + 1], c), ys.at[j + 1, c], yr.at[j + 1, c], up))
                elif c % 2 == 1:
                    go(remote(part_of(hold.at[j], c), part_of(hold.at[far - 1], c), ys.at[far - 1, c], yr.at[far - 1, c], up))
            if c == 0:
                remote(metas.at[0], metas.at[s], ms.at[base + i], mr.at[base + i], down).wait_recv()
                if s < far:
                    go(remote(metas.at[s], metas.at[s + 1], ms.at[base + i + 1], mr.at[base + i + 1], down))
                    remote(metas.at[0], metas.at[ny - s], ms.at[base + j], mr.at[base + j], up).wait_recv()
                    if s < far - 1:
                        go(remote(metas.at[ny - s], metas.at[ny - s - 1], ms.at[base + j + 1], mr.at[base + j + 1], up))
            process(2 * s - 1, c)
            if s < far:
                process(2 * s, c)
            if s == 1:
                lag.append((0, c))
            else:
                lag.append((2 * s - 3, c))
                lag.append((2 * s - 2, c))
            while lag:
                passing(*lag.pop(0))
            if ready < batches and s < far:
                upto = min(batches, ready + per)
                lax.fori_loop(ready, upto, prepare, 0)
                ready = upto
        if s == 1:
            remote(swap.at[0], across.at[0, :, first_half], sws.at[2], swr.at[2], right).wait_recv()
            remote(swap.at[1], across.at[0, :, second_half], sws.at[3], swr.at[3], left).wait_recv()
            go(remote(across.at[0], across.at[1], acs.at[0], acr.at[0], down))
            go(remote(across.at[0], across.at[1 + far], acs.at[far], acr.at[far], up))
            take(0)
        else:
            across_in(s - 1)
    for i in range(len(HOPS)):
        remote(line.at[0:4], asked.at[i], qs.at[i], qr.at[i], nears[0]).wait_recv()
    fill(0, metas[0, x, 0:1, :])
    fill(1, asked[0, 0:1, :])
    for c in range(CHUNKS):
        passing(ny - 1, c)
    for i in range(1, len(HOPS)):
        fill(1 + i, asked[i, 0:1, :])
    across_in(far)
    for g in range(ny):
        row = row_of(g) * NX
        for c in range(CHUNKS):
            remote(part_of(out_r.at[g], c), part_of(win.at[row + xl], c), rs.at[g, c], fl.at[g, c], right).wait_recv()
            remote(part_of(out_l.at[g], c), part_of(win.at[row + xr], c), ls.at[g, c], fr.at[g, c], left).wait_recv()
            some = other_part(c)
            if some is not None:
                remote(out_o.at[g, some], win.at[row + xo, some], fws.at[g, c], fo.at[g, c], right).wait_recv()

    zero = jnp.zeros((size, size), BF)
    wide = lax.broadcasted_iota(jnp.int32, (1, points), 1)
    spot = lax.broadcasted_iota(jnp.int32, (comps, 128), 1)

    def batch(b, gained):
        first = start + offsets_ref[0, b]
        places = [lax.rem(first + j, devs) for j in range(band)]

        def piece(j, k):
            return win[places[j], k]

        def quad(a, b_, c, d):
            return jnp.concatenate([jnp.concatenate([a, b_], axis=1), jnp.concatenate([c, d], axis=1)], axis=0)

        low, high = turned[b, 0 : 2 * size, :], turned[b, 2 * size : 4 * size, :]
        dot = functools.partial(jnp.dot, preferred_element_type=F32)
        m01 = dot(quad(piece(0, 1), piece(0, 2), piece(1, 0), piece(1, 1)), low)
        m01 = m01 + dot(quad(piece(0, 3), zero, piece(1, 2), piece(1, 3)), high)
        m23 = dot(quad(piece(2, 1), piece(2, 2), piece(3, 0), piece(3, 1)), high)
        m2x = dot(piece(2, 0), turned[b, size : 2 * size, :])
        density = jnp.sum(m01 * low.astype(F32) + m23 * high.astype(F32), axis=0, keepdims=True)
        density = density + jnp.sum(m2x * turned[b, 2 * size : 3 * size, :].astype(F32), axis=0, keepdims=True)
        density = jnp.where(wide < sizes_ref[0, b], density, 0.0)
        dens_ref[pl.ds(b, 1), :] = density
        for i in range(near):
            column = jnp.sum(parted[b, i] * density, axis=1, keepdims=True)
            gained = jnp.where(spot == i * batches + b, column, gained)
        return gained

    terms = lax.fori_loop(0, batches, batch, jnp.zeros((comps, 128), F32), unroll=4)
    top, low = pack(terms, pairs)
    packed[0:8] = top
    packed[8:16] = low

    sides = [{"dev": y * NX + (x + s) % NX} for s in range(1, NX)]
    for i in range(ny - 1):
        go(remote(packed, every.at[y, x], ts.at[i], tr.at[i], ups[i]))
    for i in range(NX - 1):
        go(remote(packed, every.at[y, x], xs.at[0, i], xr_.at[0, i], sides[i]))
    every[y, x] = packed[...]
    near_first = sorted(range(1, ny), key=lambda j: min(j, ny - j))

    def spread(j):
        yy = (y + ny - j) % ny
        remote(packed, every.at[yy, x], ts.at[j - 1], tr.at[j - 1], up).wait_recv()
        for i in range(NX - 1):
            go(remote(every.at[yy, x], every.at[yy, x], xs.at[j, i], xr_.at[j, i], sides[i]))

    sums[...] = jnp.zeros_like(sums)

    def collect(j):
        yy = (y + ny - j) % ny
        for i in range(NX - 1):
            xx = (x + NX - 1 - i) % NX
            remote(packed, every.at[yy, xx], xs.at[j, i], xr_.at[j, i], right).wait_recv()
        for pair in range(NX // 2):
            lefts, rights = [], []
            for xx in (2 * pair, 2 * pair + 1):
                value = unpack(every[yy, xx, 0:8], every[yy, xx, 8:16], pairs)
                high = value.astype(BF)
                lowp = (value - high.astype(F32)).astype(BF)
                lefts.append(jnp.concatenate([high, lowp], axis=0))
                rights.append(hot[yy * NX + xx])
            sums[...] += lax.dot_general(
                jnp.concatenate(lefts, axis=1), jnp.concatenate(rights, axis=1), NT, preferred_element_type=F32
            )

    for j in near_first:
        spread(j)
    collect(0)
    for j in near_first:
        collect(j)
    both = sums[0:32, :] + sums[32:64, :]
    for i in range(len(HOPS)):
        answer[i] = both[:, 128 * (i + 1) : 128 * (i + 2)]
    for i in range(len(HOPS)):
        back = {"region": (region - HOPS[i] + regions) % regions}
        go(remote(answer.at[i], got.at[i], zs.at[i], zr.at[i], back))
    moment = both[:, 0:128]
    for i in range(len(HOPS)):
        remote(answer.at[i], got.at[i], zs.at[i], zr.at[i], nears[0]).wait_recv()
        moment = moment + got[i]
    upright = jnp.concatenate([moment, jnp.zeros((96, 128), F32)], axis=0).T
    mom_ref[...] = upright[pairs : pairs + ATOM_DEV, 0:comps]
    for b in range(batches):
        gathered = jnp.zeros((comps, points), F32)
        for i in range(near):
            q = i * batches + b
            gathered = gathered + radial[b, i] * moment[0:comps, q : q + 1]
        value = jnp.sum(gathered, axis=0, keepdims=True)
        pot_ref[b : b + 1, :] = jnp.where(wide < sizes_ref[0, b], value, 0.0)
    for copy in started:
        copy.wait_send()


def hand_over(*arrays):
    def copies(*refs):
        for source, target in zip(refs[: len(arrays)], refs[len(arrays) :]):
            target[...] = source[...]

    vm = pl.BlockSpec(memory_space=pltpu.VMEM)
    return pl.pallas_call(
        copies,
        name="hand_over",
        out_shape=tuple(jax.ShapeDtypeStruct(a.shape, a.dtype) for a in arrays),
        in_specs=[vm] * len(arrays),
        out_specs=(vm,) * len(arrays),
    )(*arrays)


def per_device(
    basis_values,
    density_rows,
    block_mask,
    window_start,
    batch_offsets,
    batch_sizes,
    atom_near,
    harmonics,
    partition,
    radius,
    radial_table,
):
    devs = lax.axis_size("dev")
    ny = devs // NX
    slots, band, size, _ = density_rows.shape
    batches, near = atom_near.shape
    comps, knots = radial_table.shape
    points = basis_values.shape[2]
    dma = pltpu.SemaphoreType.DMA
    vm = pl.BlockSpec(memory_space=pltpu.VMEM)
    sm = pl.BlockSpec(memory_space=pltpu.SMEM)
    hb = pl.BlockSpec(memory_space=pl.ANY)
    block = (band, size, size)
    kept = (band, slots, size, size)
    hops = len(HOPS)
    density, moments, potential = pl.pallas_call(
        functools.partial(kernel, ny),
        name="whole_step",
        out_shape=(
            jax.ShapeDtypeStruct((batches, points), F32),
            jax.ShapeDtypeStruct((ATOM_DEV, comps), F32),
            jax.ShapeDtypeStruct((batches, points), F32),
        ),
        in_specs=[hb, sm, sm, sm, sm, vm, hb, hb, vm, hb, hb],
        out_specs=(vm, vm, vm),
        scratch_shapes=[
            pltpu.VMEM(density_rows.shape, BF),
            pltpu.VMEM(partition.shape, F32),
            pltpu.VMEM(radius.shape, F32),
            pltpu.VMEM(kept, BF),
            pltpu.VMEM((ny - 1,) + kept, BF),
            pltpu.VMEM((ny,) + block, BF),
            pltpu.VMEM((ny,) + block, BF),
            pltpu.VMEM((ny,) + block, BF),
            pltpu.VMEM((ny,) + block, BF),
            pltpu.VMEM((2, slots, size // 2, size), BF),
            pltpu.VMEM((ny, slots, size, size), BF),
            pltpu.VMEM((devs,) + block, BF),
            pltpu.VMEM((8, 128), jnp.int32),
            pltpu.VMEM((ny, NX, 4, 128), jnp.int32),
            pltpu.VMEM((hops, 4, 128), jnp.int32),
            pltpu.VMEM(basis_values.shape, BF),
            pltpu.VMEM(harmonics.shape, BF),
            pltpu.VMEM((batches, band * size, points), BF),
            pltpu.VMEM((batches, near, comps, points), F32),
            pltpu.VMEM((batches, near, comps, points), F32),
            pltpu.VMEM((16, 128), F32),
            pltpu.VMEM((ny, NX, 16, 128), F32),
            pltpu.VMEM((devs, 128 * (1 + hops), 128), BF),
            pltpu.VMEM((64, 128 * (1 + hops)), F32),
            pltpu.VMEM((hops, 32, 128), F32),
            pltpu.VMEM((hops, 32, 128), F32),
            dma((ny - 1, CHUNKS)),
            dma((ny - 1, CHUNKS)),
            dma((ny + 3,)),
            dma((ny + 3,)),
            dma((hops,)),
            dma((hops,)),
            dma((ny, CHUNKS)),
            dma((ny, CHUNKS)),
            dma((ny, CHUNKS)),
            dma((ny, CHUNKS)),
            dma((ny, CHUNKS)),
            dma((ny, CHUNKS)),
            dma((ny, CHUNKS)),
            dma((ny, CHUNKS)),
            dma((4,)),
            dma((4,)),
            dma((ny - 1,)),
            dma((ny - 1,)),
            dma((ny - 1,)),
            dma((ny - 1,)),
            dma((ny, NX - 1)),
            dma((ny, NX - 1)),
            dma((hops,)),
            dma((hops,)),
            dma((5,)),
        ],
        compiler_params=pltpu.CompilerParams(collective_id=0, has_side_effects=True),
    )(
        density_rows,
        block_mask,
        window_start,
        batch_offsets,
        batch_sizes,
        atom_near.T,
        partition,
        radius,
        radial_table.T,
        basis_values,
        harmonics,
    )
    density, moments, potential = hand_over(density, moments, potential)
    return density, moments.T, potential


def solution(mesh):
    placed = (
        P(("region", "dev"), None, None, None),
        P(("region", "dev"), None, None, None),
        P(("region", "dev"), None),
        P(("region", "dev")),
        P(("region", "dev"), None),
        P(("region", "dev"), None),
        P(("region", "dev"), None),
        P(("region", "dev"), None, None, None),
        P(("region", "dev"), None, None),
        P(("region", "dev"), None, None),
        P(),
    )
    return jax.shard_map(
        per_device,
        mesh=mesh,
        in_specs=placed,
        out_specs=(
            P(("region", "dev"), None),
            P(None, ("region", "dev")),
            P(("region", "dev"), None),
        ),
        check_vma=False,
    )
```

```python
import functools

import jax
import jax.numpy as jnp
from jax import lax
from jax.experimental import pallas as pl
from jax.experimental.pallas import tpu as pltpu
from jax.sharding import PartitionSpec as P

ATOM_DEV = 16
NX = 4
CHUNKS = 2
HOPS = (1, 2, -1, -2)
MESH = pl.DeviceIdType.MESH
NT = (((1,), (1,)), ((), ()))
TN = (((0,), (0,)), ((), ()))
F32, BF = jnp.float32, jnp.bfloat16


def remote(src, dst, send_sem, recv_sem, where):
    return pltpu.make_async_remote_copy(
        src_ref=src,
        dst_ref=dst,
        send_sem=send_sem,
        recv_sem=recv_sem,
        device_id=where,
        device_id_type=MESH,
    )


def spline_values(radii, knots):
    knot = lax.broadcasted_iota(jnp.int32, (knots, radii.shape[1]), 0).astype(F32)
    distance = jnp.abs(radii - knot)
    inner = 2.0 / 3.0 - distance * distance + 0.5 * distance * distance * distance
    rest = 2.0 - distance
    outer = rest * rest * rest * (1.0 / 6.0)
    return jnp.where(distance < 1.0, inner, jnp.where(distance < 2.0, outer, 0.0))


def pack(terms, pairs):
    lane = lax.broadcasted_iota(jnp.int32, (8, 128), 1)
    row = lax.broadcasted_iota(jnp.int32, (8, 128), 0)
    third = terms[16:24]
    last = jnp.broadcast_to(terms[24:25], (8, 128))
    top = jnp.where(lane < pairs, terms[0:8], pltpu.roll(third, 72, 1))
    tail = jnp.where(row == 0, pltpu.roll(last, 88, 1), jnp.where(row == 1, pltpu.roll(last, 48, 1), 0.0))
    low = jnp.where(lane < pairs, terms[8:16], jnp.where(lane < 88, pltpu.roll(third, 16, 1), tail))
    return top, low


def unpack(top, low, pairs):
    lane = lax.broadcasted_iota(jnp.int32, (8, 128), 1)
    row = lax.broadcasted_iota(jnp.int32, (8, 128), 0)
    live = lane < pairs
    first = jnp.where(live, top, 0.0)
    second = jnp.where(live, low, 0.0)
    third = jnp.where(lane < 56, pltpu.roll(top, 56, 1), jnp.where(live, pltpu.roll(low, 112, 1), 0.0))
    zero = jnp.broadcast_to(low[0:1], (8, 128))
    one = jnp.broadcast_to(low[1:2], (8, 128))
    last = jnp.where(lane < 40, pltpu.roll(zero, 40, 1), jnp.where(live, pltpu.roll(one, 80, 1), 0.0))
    last = jnp.where(row == 0, last, 0.0)
    return jnp.concatenate([first, second, third, last], axis=0)


def pack_sums(sums):
    lane = lax.broadcasted_iota(jnp.int32, (8, 128), 1)
    row = lax.broadcasted_iota(jnp.int32, (8, 128), 0)
    last = jnp.broadcast_to(sums[24:25], (8, 128))
    tail = jnp.where(row == 1, pltpu.roll(last, 48, 1), jnp.where(row == 2, pltpu.roll(last, 8, 1), 0.0))
    tail = jnp.where(row == 0, pltpu.roll(last, 88, 1), tail)
    return jnp.concatenate([jnp.where(lane < 88, sums[0:8], tail), sums[8:24]], axis=0)


def unpack_sums(packed):
    lane = lax.broadcasted_iota(jnp.int32, (8, 128), 1)
    row = lax.broadcasted_iota(jnp.int32, (8, 128), 0)
    lines = [jnp.broadcast_to(packed[n : n + 1], (8, 128)) for n in range(3)]
    last = jnp.where(lane < 80, pltpu.roll(lines[1], 80, 1), pltpu.roll(lines[2], 120, 1))
    last = jnp.where(lane < 40, pltpu.roll(lines[0], 40, 1), last)
    return jnp.concatenate([packed, jnp.where((row == 0) & (lane < 88), last, 0.0)], axis=0)


def kernel(
    ny,
    rows_hbm,
    mask_ref,
    start_ref,
    offsets_ref,
    sizes_ref,
    near_ref,
    part_hbm,
    radius_hbm,
    radial_ref,
    basis_hbm,
    harm_hbm,
    dens_ref,
    mom_ref,
    pot_ref,
    rows_ref,
    part_ref,
    radius_ref,
    own,
    hold,
    out_r,
    out_l,
    out_o,
    relay,
    swap,
    across,
    win,
    line,
    metas,
    asked,
    basis,
    harm,
    turned,
    parted,
    radial,
    packed,
    every,
    hot,
    sums,
    answer,
    got,
    ys,
    yr,
    ms,
    mr,
    qs,
    qr,
    rs,
    ls,
    os_,
    fr,
    fl,
    fo,
    frel,
    fws,
    sws,
    swr,
    acs,
    acr,
    ts,
    tr,
    zs,
    zr,
    local,
):
    region, me = lax.axis_index("region"), lax.axis_index("dev")
    regions, devs = lax.axis_size("region"), ny * NX
    x, y = me % NX, me // NX
    far = ny // 2
    xr, xl, xo = (x + 1) % NX, (x + NX - 1) % NX, (x + 2) % NX
    right, left, other = ({"dev": y * NX + xx} for xx in (xr, xl, xo))
    ups = [{"dev": ((y + s) % ny) * NX + x} for s in range(1, ny)]
    up, down = ups[0], ups[-1]
    nears = [{"region": (region + h + regions) % regions} for h in HOPS]
    slots, band, size, _ = rows_ref.shape
    step = band // CHUNKS
    near, batches = near_ref.shape
    pairs = near * batches
    knots, comps = radial_ref.shape
    points = part_ref.shape[2]
    started = []

    def go(copy):
        copy.start()
        started.append(copy)

    barrier = pltpu.get_barrier_semaphore()
    greeted = [up, down, right, left, other] + nears
    for peer in greeted:
        pl.semaphore_signal(barrier, inc=1, device_id=peer, device_id_type=MESH)
    fetch_rows = pltpu.make_async_copy(rows_hbm, rows_ref, local.at[2])
    fetch_rows.start()
    fetches = [
        pltpu.make_async_copy(source, target, local.at[n])
        for source, target, n in (
            (basis_hbm, basis, 0),
            (harm_hbm, harm, 1),
            (part_hbm, part_ref, 3),
            (radius_hbm, radius_ref, 4),
        )
    ]

    lane = lax.broadcasted_iota(jnp.int32, (1, 128), 1)
    line[...] = jnp.zeros_like(line)
    line[0:near, 0:batches] = near_ref[...]
    total = jnp.zeros((1, 128), jnp.int32)
    for i in range(near):
        moved = pltpu.roll(jnp.broadcast_to(line[i : i + 1, :], (8, 128)), i * batches, 1)[0:1]
        total = jnp.where((lane >= i * batches) & (lane < (i + 1) * batches), moved, total)
    atom_region = ATOM_DEV * devs
    bits = atom_region.bit_length() - 1
    side = region + lax.shift_right_logical(total, bits) - 1
    side = jnp.where(side < 0, side + regions, jnp.where(side >= regions, side - regions, side))
    target = side * atom_region + (total & (atom_region - 1))
    owned = region * atom_region + me * ATOM_DEV + lane - pairs
    whole_line = jnp.where(lane < pairs, target, jnp.where(lane < pairs + ATOM_DEV, owned, -1))
    start = start_ref[0]
    line[0:1] = whole_line
    line[1:2] = jnp.full((1, 128), start // devs, jnp.int32)
    line[2:3] = jnp.full((1, 128), start % devs, jnp.int32)
    metas[0, x] = line[0:4]
    fetch_rows.wait()
    for t in range(slots):
        for k in range(band):
            keep = jnp.full((1, 1), mask_ref[t, k], jnp.int32).astype(F32).astype(BF)
            own[k, t] = rows_ref[t, k] * keep
    pl.semaphore_wait(barrier, len(greeted))

    def part_of(ref, c):
        return ref.at[pl.ds(c * step, step)]

    for c in range(CHUNKS):
        go(remote(part_of(own, c), part_of(hold.at[0], c), ys.at[0, c], yr.at[0, c], down))
        go(remote(part_of(own, c), part_of(hold.at[far], c), ys.at[far, c], yr.at[far, c], up))
        if c == 0:
            for i, peer in enumerate((right, left, other)):
                go(remote(line.at[0:4], metas.at[0, x], ms.at[i], mr.at[i], peer))

    for copy in fetches:
        copy.start()

    def row_meta(i):
        remote(line.at[0:4], metas.at[0, (xl, xr, xo)[i]], ms.at[i], mr.at[i], right).wait_recv()

    row_meta(0)
    row_meta(1)
    lone, halfway = band - 1, size // 2
    first_half, second_half = pl.ds(0, halfway), pl.ds(halfway, halfway)
    go(remote(own.at[lone, :, first_half], swap.at[0], sws.at[0], swr.at[0], right))
    go(remote(own.at[lone, :, second_half], swap.at[1], sws.at[1], swr.at[1], left))
    base = 3

    order = [0]
    for s in range(1, far + 1):
        order.append(s)
        if s < far:
            order.append(-s)

    def row_of(g):
        return (y + order[g] + ny) % ny

    def weights(xx, d):
        q = metas[0, xx, 1:2, :]
        m = metas[0, xx, 2:3, :]
        slot = q + jnp.where(m > d, 1, 0)
        slot = jnp.where(slot >= slots, slot - slots, slot)
        return [jnp.where(slot == t, 1.0, 0.0).astype(F32).astype(BF) for t in range(slots)]

    def other_part(c):
        low, high = c * step, min((c + 1) * step, lone)
        return pl.ds(low, high - low) if high > low else None

    def straight(g, c):
        return g == ny - 1 and c == CHUNKS - 1

    def via_right(g, c):
        return (g + c) % 2 == 0

    def process(g, c, some=(0, 1, 2, 3)):
        rho = order[g]
        d = row_of(g) * NX + x
        source = own if rho == 0 else hold.at[rho - 1 if rho > 0 else far - rho - 1]
        picks = ((xr, out_r.at[g]), (xl, out_l.at[g]), (xo, out_o.at[g]), (x, win.at[d]))
        picks = [(n, (picks[n][1], weights(picks[n][0], d))) for n in some]
        for k in range(c * step, (c + 1) * step):
            parts = [source[k, t] for t in range(slots)]
            for n, (dst, w) in picks:
                if n == 2 and k == lone:
                    continue
                chosen = parts[0] * w[0]
                for t in range(1, slots):
                    chosen = chosen + parts[t] * w[t]
                dst[k] = chosen
        if 2 in some and other_part(c) is not None:
            piece = other_part(c)
            if straight(g, c):
                go(remote(out_o.at[g, piece], win.at[d, piece], os_.at[g, c], fo.at[g, c], other))
            else:
                go(remote(out_o.at[g, piece], relay.at[g, piece], os_.at[g, c], frel.at[g, c], right if via_right(g, c) else left))
        if 0 not in some:
            return
        go(remote(part_of(out_r.at[g], c), part_of(win.at[d], c), rs.at[g, c], fl.at[g, c], right))
        go(remote(part_of(out_l.at[g], c), part_of(win.at[d], c), ls.at[g, c], fr.at[g, c], left))

    def passing(g, c):
        some = other_part(c)
        if some is None or straight(g, c):
            return
        toward, origin = (right, xl) if via_right(g, c) else (left, xr)
        d = row_of(g) * NX + origin
        remote(out_o.at[g, some], relay.at[g, some], os_.at[g, c], frel.at[g, c], right).wait_recv()
        go(remote(relay.at[g, some], win.at[d, some], fws.at[g, c], fo.at[g, c], toward))

    def take(g):
        rho = order[g]
        d = row_of(g) * NX + xo
        source = across.at[0 if rho == 0 else (rho if rho > 0 else far - rho)]
        w = weights(x, d)
        chosen = source[0] * w[0]
        for t in range(1, slots):
            chosen = chosen + source[t] * w[t]
        win[d, lone] = chosen

    def across_in(s):
        i, j = s - 1, far + s - 1
        remote(across.at[0], across.at[1 + i], acs.at[i], acr.at[i], down).wait_recv()
        if s < far:
            go(remote(across.at[1 + i], across.at[2 + i], acs.at[i + 1], acr.at[i + 1], down))
            remote(across.at[0], across.at[1 + j], acs.at[j], acr.at[j], up).wait_recv()
            if s < far - 1:
                go(remote(across.at[1 + j], across.at[2 + j], acs.at[j + 1], acr.at[j + 1], up))
        take(2 * s - 1)
        if s < far:
            take(2 * s)

    def prepare(b, carry):
        for j in range(band):
            turned[b, j * size : (j + 1) * size, :] = basis[b, j].T
        for i in range(near):
            values = harm[b, i].astype(F32)
            parted[b, i] = values * part_ref[b, i : i + 1, :]
            spline = spline_values(radius_ref[b, i : i + 1, :], knots)
            curve = lax.dot_general(
                radial_ref[...], spline, TN, precision=lax.Precision.HIGHEST, preferred_element_type=F32
            )
            radial[b, i] = values * curve
        return carry

    def fill(h):
        def each(dx, carry):
            xx = lax.rem(x + dx, NX)
            asked_line = metas[0, xx, 0:1, :] if h == 0 else asked[h - 1, xx, 0:1, :]
            column = jnp.broadcast_to(asked_line, (128, 128)).T

            def one(rho, inner):
                same = jnp.where(column == metas[rho, x, 0:1, :], 1.0, 0.0).astype(F32)
                hot[rho, pl.ds((h * NX + dx) * 128, 128), :] = same.astype(BF)
                return inner

            return lax.fori_loop(0, ny, one, carry)

        lax.fori_loop(0, NX, each, 0)

    for c in range(CHUNKS):
        process(0, c, (0, 1))
    row_meta(2)
    for i in range(len(HOPS)):
        go(remote(metas.at[0], asked.at[i], qs.at[i], qr.at[i], nears[i]))
    go(remote(metas.at[0], metas.at[1], ms.at[base], mr.at[base], down))
    go(remote(metas.at[0], metas.at[ny - 1], ms.at[base + far], mr.at[base + far], up))
    for c in range(CHUNKS):
        process(0, c, (2, 3))
    remote(own.at[lone, :, first_half], swap.at[0], sws.at[0], swr.at[0], right).wait_recv()
    go(remote(swap.at[0], across.at[0, :, first_half], sws.at[2], swr.at[2], right))
    remote(own.at[lone, :, second_half], swap.at[1], sws.at[1], swr.at[1], left).wait_recv()
    go(remote(swap.at[1], across.at[0, :, second_half], sws.at[3], swr.at[3], left))
    for copy in fetches:
        copy.wait()
    per = -(-batches // (CHUNKS * (far - 1)))
    ready = 0
    lag = []
    for s in range(1, far + 1):
        i, j = s - 1, far + s - 1
        for c in range(CHUNKS):
            remote(part_of(own, c), part_of(hold.at[i], c), ys.at[i, c], yr.at[i, c], down).wait_recv()
            if s < far - 1 or (s < far and c % 2 == 0):
                go(remote(part_of(hold.at[i], c), part_of(hold.at[i + 1], c), ys.at[i + 1, c], yr.at[i + 1, c], down))
            if s < far:
                remote(part_of(own, c), part_of(hold.at[j], c), ys.at[j, c], yr.at[j, c], up).wait_recv()
                if s < far - 1:
                    go(remote(part_of(hold.at[j], c), part_of(hold.at[j + 1], c), ys.at[j + 1, c], yr.at[j + 1, c], up))
                elif c % 2 == 1:
                    go(remote(part_of(hold.at[j], c), part_of(hold.at[far - 1], c), ys.at[far - 1, c], yr.at[far - 1, c], up))
            if c == 0:
                remote(metas.at[0], metas.at[s], ms.at[base + i], mr.at[base + i], down).wait_recv()
                if s < far:
                    go(remote(metas.at[s], metas.at[s + 1], ms.at[base + i + 1], mr.at[base + i + 1], down))
                    remote(metas.at[0], metas.at[ny - s], ms.at[base + j], mr.at[base + j], up).wait_recv()
                    if s < far - 1:
                        go(remote(metas.at[ny - s], metas.at[ny - s - 1], ms.at[base + j + 1], mr.at[base + j + 1], up))
            process(2 * s - 1, c)
            if s < far:
                process(2 * s, c)
            if s == 1:
                lag.append((0, c))
            else:
                lag.append((2 * s - 3, c))
                lag.append((2 * s - 2, c))
            while lag:
                passing(*lag.pop(0))
            if ready < batches and s < far:
                upto = min(batches, ready + per)
                lax.fori_loop(ready, upto, prepare, 0)
                ready = upto
        if s == 1:
            remote(swap.at[0], across.at[0, :, first_half], sws.at[2], swr.at[2], right).wait_recv()
            remote(swap.at[1], across.at[0, :, second_half], sws.at[3], swr.at[3], left).wait_recv()
            go(remote(across.at[0], across.at[1], acs.at[0], acr.at[0], down))
            go(remote(across.at[0], across.at[1 + far], acs.at[far], acr.at[far], up))
            take(0)
        else:
            across_in(s - 1)
    for i in range(len(HOPS)):
        remote(metas.at[0], asked.at[i], qs.at[i], qr.at[i], nears[0]).wait_recv()
    fill(0)
    fill(1)
    for c in range(CHUNKS):
        passing(ny - 1, c)
    for i in range(1, len(HOPS)):
        fill(1 + i)
    across_in(far)
    for g in range(ny):
        row = row_of(g) * NX
        for c in range(CHUNKS):
            remote(part_of(out_r.at[g], c), part_of(win.at[row + xl], c), rs.at[g, c], fl.at[g, c], right).wait_recv()
            remote(part_of(out_l.at[g], c), part_of(win.at[row + xr], c), ls.at[g, c], fr.at[g, c], left).wait_recv()
            some = other_part(c)
            if some is not None:
                remote(out_o.at[g, some], win.at[row + xo, some], fws.at[g, c], fo.at[g, c], right).wait_recv()

    zero = jnp.zeros((size, size), BF)
    wide = lax.broadcasted_iota(jnp.int32, (1, points), 1)
    spot = lax.broadcasted_iota(jnp.int32, (comps, 128), 1)

    def batch(b, gained):
        first = start + offsets_ref[0, b]
        places = [lax.rem(first + j, devs) for j in range(band)]

        def piece(j, k):
            return win[places[j], k]

        def quad(a, b_, c, d):
            return jnp.concatenate([jnp.concatenate([a, b_], axis=1), jnp.concatenate([c, d], axis=1)], axis=0)

        low, high = turned[b, 0 : 2 * size, :], turned[b, 2 * size : 4 * size, :]
        dot = functools.partial(jnp.dot, preferred_element_type=F32)
        m01 = dot(quad(piece(0, 1), piece(0, 2), piece(1, 0), piece(1, 1)), low)
        m01 = m01 + dot(quad(piece(0, 3), zero, piece(1, 2), piece(1, 3)), high)
        m23 = dot(quad(piece(2, 1), piece(2, 2), piece(3, 0), piece(3, 1)), high)
        m2x = dot(piece(2, 0), turned[b, size : 2 * size, :])
        density = jnp.sum(m01 * low.astype(F32) + m23 * high.astype(F32), axis=0, keepdims=True)
        density = density + jnp.sum(m2x * turned[b, 2 * size : 3 * size, :].astype(F32), axis=0, keepdims=True)
        density = jnp.where(wide < sizes_ref[0, b], density, 0.0)
        dens_ref[pl.ds(b, 1), :] = density
        for i in range(near):
            column = jnp.sum(parted[b, i] * density, axis=1, keepdims=True)
            gained = jnp.where(spot == i * batches + b, column, gained)
        return gained

    terms = lax.fori_loop(0, batches, batch, jnp.zeros((comps, 128), F32), unroll=4)
    top, low = pack(terms, pairs)
    packed[0:8] = top
    packed[8:16] = low

    for i in range(ny - 1):
        go(remote(packed, every.at[i + 1], ts.at[i], tr.at[i], ups[i]))
    every[0] = packed[...]
    turns = [0] + sorted(range(1, ny), key=lambda j: min(j, ny - j))
    sums[...] = jnp.zeros_like(sums)
    for pair in range(ny // 2):
        lefts, rights = [], []
        for j in turns[2 * pair : 2 * pair + 2]:
            if j:
                remote(packed, every.at[j], ts.at[j - 1], tr.at[j - 1], up).wait_recv()
            value = unpack(every[j, 0:8], every[j, 8:16], pairs)
            high = value.astype(BF)
            rest = (value - high.astype(F32)).astype(BF)
            lefts.append(jnp.concatenate([high, rest], axis=0))
            rights.append(hot[(ny - j) % ny])
        sums[...] += lax.dot_general(
            jnp.concatenate(lefts, axis=1), jnp.concatenate(rights, axis=1), NT, preferred_element_type=F32
        )

    def answers_of(slot):
        lanes = slice(128 * slot, 128 * (slot + 1))
        return pack_sums(sums[0:32, lanes] + sums[32:64, lanes])

    far_first = sorted(range(1, NX * (1 + len(HOPS))), key=lambda n: -(min(n % NX, NX - n % NX) + (n >= NX)))
    for slot in far_first:
        h, dx = slot // NX, slot % NX
        answer[slot] = answers_of(slot)
        where = {"dev": y * NX + (x + dx) % NX}
        if h:
            where["region"] = (region - HOPS[h - 1] + regions) % regions
        go(remote(answer.at[slot], got.at[slot], zs.at[slot], zr.at[slot], where))
    gained = answers_of(0)
    for slot in reversed(far_first):
        remote(answer.at[slot], got.at[slot], zs.at[slot], zr.at[slot], right).wait_recv()
        gained = gained + got[slot]
    moment = unpack_sums(gained)
    upright = jnp.concatenate([moment, jnp.zeros((96, 128), F32)], axis=0).T
    mom_ref[...] = upright[pairs : pairs + ATOM_DEV, 0:comps]
    for b in range(batches):
        gathered = jnp.zeros((comps, points), F32)
        for i in range(near):
            q = i * batches + b
            gathered = gathered + radial[b, i] * moment[0:comps, q : q + 1]
        value = jnp.sum(gathered, axis=0, keepdims=True)
        pot_ref[b : b + 1, :] = jnp.where(wide < sizes_ref[0, b], value, 0.0)
    for copy in started:
        copy.wait_send()


def hand_over(*arrays):
    def copies(*refs):
        for source, target in zip(refs[: len(arrays)], refs[len(arrays) :]):
            target[...] = source[...]

    vm = pl.BlockSpec(memory_space=pltpu.VMEM)
    return pl.pallas_call(
        copies,
        name="hand_over",
        out_shape=tuple(jax.ShapeDtypeStruct(a.shape, a.dtype) for a in arrays),
        in_specs=[vm] * len(arrays),
        out_specs=(vm,) * len(arrays),
    )(*arrays)


def per_device(
    basis_values,
    density_rows,
    block_mask,
    window_start,
    batch_offsets,
    batch_sizes,
    atom_near,
    harmonics,
    partition,
    radius,
    radial_table,
):
    devs = lax.axis_size("dev")
    ny = devs // NX
    slots, band, size, _ = density_rows.shape
    batches, near = atom_near.shape
    comps, knots = radial_table.shape
    points = basis_values.shape[2]
    dma = pltpu.SemaphoreType.DMA
    vm = pl.BlockSpec(memory_space=pltpu.VMEM)
    sm = pl.BlockSpec(memory_space=pltpu.SMEM)
    hb = pl.BlockSpec(memory_space=pl.ANY)
    block = (band, size, size)
    kept = (band, slots, size, size)
    hops = len(HOPS)
    density, moments, potential = pl.pallas_call(
        functools.partial(kernel, ny),
        name="whole_step",
        out_shape=(
            jax.ShapeDtypeStruct((batches, points), F32),
            jax.ShapeDtypeStruct((ATOM_DEV, comps), F32),
            jax.ShapeDtypeStruct((batches, points), F32),
        ),
        in_specs=[hb, sm, sm, sm, sm, vm, hb, hb, vm, hb, hb],
        out_specs=(vm, vm, vm),
        scratch_shapes=[
            pltpu.VMEM(density_rows.shape, BF),
            pltpu.VMEM(partition.shape, F32),
            pltpu.VMEM(radius.shape, F32),
            pltpu.VMEM(kept, BF),
            pltpu.VMEM((ny - 1,) + kept, BF),
            pltpu.VMEM((ny,) + block, BF),
            pltpu.VMEM((ny,) + block, BF),
            pltpu.VMEM((ny,) + block, BF),
            pltpu.VMEM((ny,) + block, BF),
            pltpu.VMEM((2, slots, size // 2, size), BF),
            pltpu.VMEM((ny, slots, size, size), BF),
            pltpu.VMEM((devs,) + block, BF),
            pltpu.VMEM((8, 128), jnp.int32),
            pltpu.VMEM((ny, NX, 4, 128), jnp.int32),
            pltpu.VMEM((hops, NX, 4, 128), jnp.int32),
            pltpu.VMEM(basis_values.shape, BF),
            pltpu.VMEM(harmonics.shape, BF),
            pltpu.VMEM((batches, band * size, points), BF),
            pltpu.VMEM((batches, near, comps, points), F32),
            pltpu.VMEM((batches, near, comps, points), F32),
            pltpu.VMEM((16, 128), F32),
            pltpu.VMEM((ny, 16, 128), F32),
            pltpu.VMEM((ny, 128 * NX * (1 + hops), 128), BF),
            pltpu.VMEM((64, 128 * NX * (1 + hops)), F32),
            pltpu.VMEM((NX * (1 + hops), 24, 128), F32),
            pltpu.VMEM((NX * (1 + hops), 24, 128), F32),
            dma((ny - 1, CHUNKS)),
            dma((ny - 1, CHUNKS)),
            dma((ny + 3,)),
            dma((ny + 3,)),
            dma((hops,)),
            dma((hops,)),
            dma((ny, CHUNKS)),
            dma((ny, CHUNKS)),
            dma((ny, CHUNKS)),
            dma((ny, CHUNKS)),
            dma((ny, CHUNKS)),
            dma((ny, CHUNKS)),
            dma((ny, CHUNKS)),
            dma((ny, CHUNKS)),
            dma((4,)),
            dma((4,)),
            dma((ny - 1,)),
            dma((ny - 1,)),
            dma((ny - 1,)),
            dma((ny - 1,)),
            dma((NX * (1 + hops),)),
            dma((NX * (1 + hops),)),
            dma((5,)),
        ],
        compiler_params=pltpu.CompilerParams(collective_id=0, has_side_effects=True),
    )(
        density_rows,
        block_mask,
        window_start,
        batch_offsets,
        batch_sizes,
        atom_near.T,
        partition,
        radius,
        radial_table.T,
        basis_values,
        harmonics,
    )
    density, moments, potential = hand_over(density, moments, potential)
    return density, moments.T, potential


def solution(mesh):
    placed = (
        P(("region", "dev"), None, None, None),
        P(("region", "dev"), None, None, None),
        P(("region", "dev"), None),
        P(("region", "dev")),
        P(("region", "dev"), None),
        P(("region", "dev"), None),
        P(("region", "dev"), None),
        P(("region", "dev"), None, None, None),
        P(("region", "dev"), None, None),
        P(("region", "dev"), None, None),
        P(),
    )
    return jax.shard_map(
        per_device,
        mesh=mesh,
        in_specs=placed,
        out_specs=(
            P(("region", "dev"), None),
            P(None, ("region", "dev")),
            P(("region", "dev"), None),
        ),
        check_vma=False,
    )
```

```python
import functools

import jax
import jax.numpy as jnp
from jax import lax
from jax.experimental import pallas as pl
from jax.experimental.pallas import tpu as pltpu
from jax.sharding import PartitionSpec as P

ATOM_DEV = 16
NX = 4
CHUNKS = 2
HOPS = (1, 2, -1, -2)
MESH = pl.DeviceIdType.MESH
TN = (((0,), (0,)), ((), ()))
F32, BF = jnp.float32, jnp.bfloat16


def remote(src, dst, send_sem, recv_sem, where):
    return pltpu.make_async_remote_copy(
        src_ref=src,
        dst_ref=dst,
        send_sem=send_sem,
        recv_sem=recv_sem,
        device_id=where,
        device_id_type=MESH,
    )


def spline_values(radii, knots):
    knot = lax.broadcasted_iota(jnp.int32, (knots, radii.shape[1]), 0).astype(F32)
    distance = jnp.abs(radii - knot)
    inner = 2.0 / 3.0 - distance * distance + 0.5 * distance * distance * distance
    rest = 2.0 - distance
    outer = rest * rest * rest * (1.0 / 6.0)
    return jnp.where(distance < 1.0, inner, jnp.where(distance < 2.0, outer, 0.0))


def pack(terms, pairs):
    lane = lax.broadcasted_iota(jnp.int32, (8, 128), 1)
    row = lax.broadcasted_iota(jnp.int32, (8, 128), 0)
    third = terms[16:24]
    last = jnp.broadcast_to(terms[24:25], (8, 128))
    top = jnp.where(lane < pairs, terms[0:8], pltpu.roll(third, 72, 1))
    tail = jnp.where(row == 0, pltpu.roll(last, 88, 1), jnp.where(row == 1, pltpu.roll(last, 48, 1), 0.0))
    low = jnp.where(lane < pairs, terms[8:16], jnp.where(lane < 88, pltpu.roll(third, 16, 1), tail))
    return top, low


def unpack(top, low, pairs):
    lane = lax.broadcasted_iota(jnp.int32, (8, 128), 1)
    row = lax.broadcasted_iota(jnp.int32, (8, 128), 0)
    live = lane < pairs
    first = jnp.where(live, top, 0.0)
    second = jnp.where(live, low, 0.0)
    third = jnp.where(lane < 56, pltpu.roll(top, 56, 1), jnp.where(live, pltpu.roll(low, 112, 1), 0.0))
    zero = jnp.broadcast_to(low[0:1], (8, 128))
    one = jnp.broadcast_to(low[1:2], (8, 128))
    last = jnp.where(lane < 40, pltpu.roll(zero, 40, 1), jnp.where(live, pltpu.roll(one, 80, 1), 0.0))
    last = jnp.where(row == 0, last, 0.0)
    return jnp.concatenate([first, second, third, last], axis=0)


def pack_sums(sums):
    lane = lax.broadcasted_iota(jnp.int32, (8, 128), 1)
    row = lax.broadcasted_iota(jnp.int32, (8, 128), 0)
    last = jnp.broadcast_to(sums[24:25], (8, 128))
    tail = jnp.where(row == 1, pltpu.roll(last, 48, 1), jnp.where(row == 2, pltpu.roll(last, 8, 1), 0.0))
    tail = jnp.where(row == 0, pltpu.roll(last, 88, 1), tail)
    return jnp.concatenate([jnp.where(lane < 88, sums[0:8], tail), sums[8:24]], axis=0)


def unpack_sums(packed):
    lane = lax.broadcasted_iota(jnp.int32, (8, 128), 1)
    row = lax.broadcasted_iota(jnp.int32, (8, 128), 0)
    lines = [jnp.broadcast_to(packed[n : n + 1], (8, 128)) for n in range(3)]
    last = jnp.where(lane < 80, pltpu.roll(lines[1], 80, 1), pltpu.roll(lines[2], 120, 1))
    last = jnp.where(lane < 40, pltpu.roll(lines[0], 40, 1), last)
    return jnp.concatenate([packed, jnp.where((row == 0) & (lane < 88), last, 0.0)], axis=0)


def kernel(
    ny,
    rows_hbm,
    mask_ref,
    start_ref,
    offsets_ref,
    sizes_ref,
    near_ref,
    part_hbm,
    radius_hbm,
    radial_ref,
    basis_hbm,
    harm_hbm,
    dens_ref,
    mom_ref,
    pot_ref,
    rows_ref,
    part_ref,
    radius_ref,
    own,
    hold,
    out_r,
    out_l,
    out_o,
    relay,
    swap,
    across,
    win,
    line,
    metas,
    asked,
    basis,
    harm,
    turned,
    parted,
    radial,
    packed,
    every,
    hot,
    sums,
    answer,
    got,
    ys,
    yr,
    ms,
    mr,
    qs,
    qr,
    rs,
    ls,
    os_,
    fr,
    fl,
    fo,
    frel,
    fws,
    sws,
    swr,
    acs,
    acr,
    ts,
    tr,
    zs,
    zr,
    local,
):
    region, me = lax.axis_index("region"), lax.axis_index("dev")
    regions, devs = lax.axis_size("region"), ny * NX
    x, y = me % NX, me // NX
    far = ny // 2
    xr, xl, xo = (x + 1) % NX, (x + NX - 1) % NX, (x + 2) % NX
    right, left, other = ({"dev": y * NX + xx} for xx in (xr, xl, xo))
    ups = [{"dev": ((y + s) % ny) * NX + x} for s in range(1, ny)]
    up, down = ups[0], ups[-1]
    nears = [{"region": (region + h + regions) % regions} for h in HOPS]
    slots, band, size, _ = rows_ref.shape
    step = band // CHUNKS
    near, batches = near_ref.shape
    pairs = near * batches
    knots, comps = radial_ref.shape
    points = part_ref.shape[2]
    started = []

    def go(copy):
        copy.start()
        started.append(copy)

    barrier = pltpu.get_barrier_semaphore()
    greeted = [up, down, right, left, other] + nears
    for peer in greeted:
        pl.semaphore_signal(barrier, inc=1, device_id=peer, device_id_type=MESH)
    fetch_rows = pltpu.make_async_copy(rows_hbm, rows_ref, local.at[2])
    fetch_rows.start()
    fetches = [
        pltpu.make_async_copy(source, target, local.at[n])
        for source, target, n in (
            (basis_hbm, basis, 0),
            (harm_hbm, harm, 1),
            (part_hbm, part_ref, 3),
            (radius_hbm, radius_ref, 4),
        )
    ]

    lane = lax.broadcasted_iota(jnp.int32, (1, 128), 1)
    line[...] = jnp.zeros_like(line)
    line[0:near, 0:batches] = near_ref[...]
    total = jnp.zeros((1, 128), jnp.int32)
    for i in range(near):
        moved = pltpu.roll(jnp.broadcast_to(line[i : i + 1, :], (8, 128)), i * batches, 1)[0:1]
        total = jnp.where((lane >= i * batches) & (lane < (i + 1) * batches), moved, total)
    atom_region = ATOM_DEV * devs
    bits = atom_region.bit_length() - 1
    side = region + lax.shift_right_logical(total, bits) - 1
    side = jnp.where(side < 0, side + regions, jnp.where(side >= regions, side - regions, side))
    target = side * atom_region + (total & (atom_region - 1))
    owned = region * atom_region + me * ATOM_DEV + lane - pairs
    whole_line = jnp.where(lane < pairs, target, jnp.where(lane < pairs + ATOM_DEV, owned, -1))
    start = start_ref[0]
    line[0:1] = whole_line
    line[1:2] = jnp.full((1, 128), start // devs, jnp.int32)
    line[2:3] = jnp.full((1, 128), start % devs, jnp.int32)
    metas[0, x] = line[0:4]
    fetch_rows.wait()
    for t in range(slots):
        for k in range(band):
            keep = jnp.full((1, 1), mask_ref[t, k], jnp.int32).astype(F32).astype(BF)
            own[k, t] = rows_ref[t, k] * keep
    pl.semaphore_wait(barrier, len(greeted))

    def part_of(ref, c):
        return ref.at[pl.ds(c * step, step)]

    for c in range(CHUNKS):
        go(remote(part_of(own, c), part_of(hold.at[0], c), ys.at[0, c], yr.at[0, c], down))
        go(remote(part_of(own, c), part_of(hold.at[far], c), ys.at[far, c], yr.at[far, c], up))
        if c == 0:
            for i, peer in enumerate((right, left, other)):
                go(remote(line.at[0:4], metas.at[0, x], ms.at[i], mr.at[i], peer))

    for copy in fetches:
        copy.start()

    def row_meta(i):
        remote(line.at[0:4], metas.at[0, (xl, xr, xo)[i]], ms.at[i], mr.at[i], right).wait_recv()

    row_meta(0)
    row_meta(1)
    lone, halfway = band - 1, size // 2
    first_half, second_half = pl.ds(0, halfway), pl.ds(halfway, halfway)
    go(remote(own.at[lone, :, first_half], swap.at[0], sws.at[0], swr.at[0], right))
    go(remote(own.at[lone, :, second_half], swap.at[1], sws.at[1], swr.at[1], left))
    base = 3

    order = [0]
    for s in range(1, far + 1):
        order.append(s)
        if s < far:
            order.append(-s)

    def row_of(g):
        return (y + order[g] + ny) % ny

    def weights(xx, d):
        q = metas[0, xx, 1:2, :]
        m = metas[0, xx, 2:3, :]
        slot = q + jnp.where(m > d, 1, 0)
        slot = jnp.where(slot >= slots, slot - slots, slot)
        return [jnp.where(slot == t, 1.0, 0.0).astype(F32).astype(BF) for t in range(slots)]

    def other_part(c):
        low, high = c * step, min((c + 1) * step, lone)
        return pl.ds(low, high - low) if high > low else None

    def straight(g, c):
        return g == ny - 1 and c == CHUNKS - 1

    def via_right(g, c):
        return (g + c) % 2 == 0

    def process(g, c, some=(0, 1, 2, 3)):
        rho = order[g]
        d = row_of(g) * NX + x
        source = own if rho == 0 else hold.at[rho - 1 if rho > 0 else far - rho - 1]
        picks = ((xr, out_r.at[g]), (xl, out_l.at[g]), (xo, out_o.at[g]), (x, win.at[d]))
        picks = [(n, (picks[n][1], weights(picks[n][0], d))) for n in some]
        for k in range(c * step, (c + 1) * step):
            parts = [source[k, t] for t in range(slots)]
            for n, (dst, w) in picks:
                if n == 2 and k == lone:
                    continue
                chosen = parts[0] * w[0]
                for t in range(1, slots):
                    chosen = chosen + parts[t] * w[t]
                dst[k] = chosen
        if 2 in some and other_part(c) is not None:
            piece = other_part(c)
            if straight(g, c):
                go(remote(out_o.at[g, piece], win.at[d, piece], os_.at[g, c], fo.at[g, c], other))
            else:
                go(remote(out_o.at[g, piece], relay.at[g, piece], os_.at[g, c], frel.at[g, c], right if via_right(g, c) else left))
        if 0 not in some:
            return
        go(remote(part_of(out_r.at[g], c), part_of(win.at[d], c), rs.at[g, c], fl.at[g, c], right))
        go(remote(part_of(out_l.at[g], c), part_of(win.at[d], c), ls.at[g, c], fr.at[g, c], left))

    def passing(g, c):
        some = other_part(c)
        if some is None or straight(g, c):
            return
        toward, origin = (right, xl) if via_right(g, c) else (left, xr)
        d = row_of(g) * NX + origin
        remote(out_o.at[g, some], relay.at[g, some], os_.at[g, c], frel.at[g, c], right).wait_recv()
        go(remote(relay.at[g, some], win.at[d, some], fws.at[g, c], fo.at[g, c], toward))

    def take(g):
        rho = order[g]
        d = row_of(g) * NX + xo
        source = across.at[0 if rho == 0 else (rho if rho > 0 else far - rho)]
        w = weights(x, d)
        chosen = source[0] * w[0]
        for t in range(1, slots):
            chosen = chosen + source[t] * w[t]
        win[d, lone] = chosen

    def across_in(s):
        i, j = s - 1, far + s - 1
        remote(across.at[0], across.at[1 + i], acs.at[i], acr.at[i], down).wait_recv()
        if s < far:
            go(remote(across.at[1 + i], across.at[2 + i], acs.at[i + 1], acr.at[i + 1], down))
            remote(across.at[0], across.at[1 + j], acs.at[j], acr.at[j], up).wait_recv()
            if s < far - 1:
                go(remote(across.at[1 + j], across.at[2 + j], acs.at[j + 1], acr.at[j + 1], up))
        take(2 * s - 1)
        if s < far:
            take(2 * s)

    def prepare(b, carry):
        for j in range(band):
            turned[b, j * size : (j + 1) * size, :] = basis[b, j].T
        for i in range(near):
            values = harm[b, i].astype(F32)
            parted[b, i] = values * part_ref[b, i : i + 1, :]
            spline = spline_values(radius_ref[b, i : i + 1, :], knots)
            curve = lax.dot_general(
                radial_ref[...], spline, TN, precision=lax.Precision.HIGHEST, preferred_element_type=F32
            )
            radial[b, i] = values * curve
        return carry

    def fill(some):
        def one(rho, carry):
            column = jnp.broadcast_to(metas[rho, x, 0:1, :], (128, 128)).T
            for h in some:
                for dx in range(NX):
                    xx = (x + dx) % NX
                    line_of = metas[0, xx, 0:1, :] if h == 0 else asked[h - 1, xx, 0:1, :]
                    same = jnp.where(column == line_of, 1.0, 0.0).astype(F32)
                    slot = h * NX + dx
                    hot[rho, :, 128 * slot : 128 * (slot + 1)] = same.astype(BF)
            return carry

        lax.fori_loop(0, ny, one, 0)

    for c in range(CHUNKS):
        process(0, c, (0, 1))
    row_meta(2)
    for i in range(len(HOPS)):
        go(remote(metas.at[0], asked.at[i], qs.at[i], qr.at[i], nears[i]))
    go(remote(metas.at[0], metas.at[1], ms.at[base], mr.at[base], down))
    go(remote(metas.at[0], metas.at[ny - 1], ms.at[base + far], mr.at[base + far], up))
    for c in range(CHUNKS):
        process(0, c, (2, 3))
    remote(own.at[lone, :, first_half], swap.at[0], sws.at[0], swr.at[0], right).wait_recv()
    go(remote(swap.at[0], across.at[0, :, first_half], sws.at[2], swr.at[2], right))
    remote(own.at[lone, :, second_half], swap.at[1], sws.at[1], swr.at[1], left).wait_recv()
    go(remote(swap.at[1], across.at[0, :, second_half], sws.at[3], swr.at[3], left))
    for copy in fetches:
        copy.wait()
    per = -(-batches // (CHUNKS * (far - 1)))
    ready = 0
    lag = []
    for s in range(1, far + 1):
        i, j = s - 1, far + s - 1
        for c in range(CHUNKS):
            remote(part_of(own, c), part_of(hold.at[i], c), ys.at[i, c], yr.at[i, c], down).wait_recv()
            if s < far - 1 or (s < far and c % 2 == 0):
                go(remote(part_of(hold.at[i], c), part_of(hold.at[i + 1], c), ys.at[i + 1, c], yr.at[i + 1, c], down))
            if s < far:
                remote(part_of(own, c), part_of(hold.at[j], c), ys.at[j, c], yr.at[j, c], up).wait_recv()
                if s < far - 1:
                    go(remote(part_of(hold.at[j], c), part_of(hold.at[j + 1], c), ys.at[j + 1, c], yr.at[j + 1, c], up))
                elif c % 2 == 1:
                    go(remote(part_of(hold.at[j], c), part_of(hold.at[far - 1], c), ys.at[far - 1, c], yr.at[far - 1, c], up))
            if c == 0:
                remote(metas.at[0], metas.at[s], ms.at[base + i], mr.at[base + i], down).wait_recv()
                if s < far:
                    go(remote(metas.at[s], metas.at[s + 1], ms.at[base + i + 1], mr.at[base + i + 1], down))
                    remote(metas.at[0], metas.at[ny - s], ms.at[base + j], mr.at[base + j], up).wait_recv()
                    if s < far - 1:
                        go(remote(metas.at[ny - s], metas.at[ny - s - 1], ms.at[base + j + 1], mr.at[base + j + 1], up))
            process(2 * s - 1, c)
            if s < far:
                process(2 * s, c)
            if s == 1:
                lag.append((0, c))
            else:
                lag.append((2 * s - 3, c))
                lag.append((2 * s - 2, c))
            while lag:
                passing(*lag.pop(0))
            if ready < batches and s < far:
                upto = min(batches, ready + per)
                lax.fori_loop(ready, upto, prepare, 0)
                ready = upto
        if s == 1:
            remote(swap.at[0], across.at[0, :, first_half], sws.at[2], swr.at[2], right).wait_recv()
            remote(swap.at[1], across.at[0, :, second_half], sws.at[3], swr.at[3], left).wait_recv()
            go(remote(across.at[0], across.at[1], acs.at[0], acr.at[0], down))
            go(remote(across.at[0], across.at[1 + far], acs.at[far], acr.at[far], up))
            take(0)
        else:
            across_in(s - 1)
    for i in range(len(HOPS)):
        remote(metas.at[0], asked.at[i], qs.at[i], qr.at[i], nears[0]).wait_recv()
    fill((0, 1))
    for c in range(CHUNKS):
        passing(ny - 1, c)
    fill(tuple(range(2, 1 + len(HOPS))))
    across_in(far)
    for g in range(ny):
        row = row_of(g) * NX
        for c in range(CHUNKS):
            remote(part_of(out_r.at[g], c), part_of(win.at[row + xl], c), rs.at[g, c], fl.at[g, c], right).wait_recv()
            remote(part_of(out_l.at[g], c), part_of(win.at[row + xr], c), ls.at[g, c], fr.at[g, c], left).wait_recv()
            some = other_part(c)
            if some is not None:
                remote(out_o.at[g, some], win.at[row + xo, some], fws.at[g, c], fo.at[g, c], right).wait_recv()

    zero = jnp.zeros((size, size), BF)
    wide = lax.broadcasted_iota(jnp.int32, (1, points), 1)
    spot = lax.broadcasted_iota(jnp.int32, (comps, 128), 1)

    def batch(b, gained):
        first = start + offsets_ref[0, b]
        places = [lax.rem(first + j, devs) for j in range(band)]

        def piece(j, k):
            return win[places[j], k]

        def quad(a, b_, c, d):
            return jnp.concatenate([jnp.concatenate([a, b_], axis=1), jnp.concatenate([c, d], axis=1)], axis=0)

        low, high = turned[b, 0 : 2 * size, :], turned[b, 2 * size : 4 * size, :]
        dot = functools.partial(jnp.dot, preferred_element_type=F32)
        m01 = dot(quad(piece(0, 1), piece(0, 2), piece(1, 0), piece(1, 1)), low)
        m01 = m01 + dot(quad(piece(0, 3), zero, piece(1, 2), piece(1, 3)), high)
        m23 = dot(quad(piece(2, 1), piece(2, 2), piece(3, 0), piece(3, 1)), high)
        m2x = dot(piece(2, 0), turned[b, size : 2 * size, :])
        density = jnp.sum(m01 * low.astype(F32) + m23 * high.astype(F32), axis=0, keepdims=True)
        density = density + jnp.sum(m2x * turned[b, 2 * size : 3 * size, :].astype(F32), axis=0, keepdims=True)
        density = jnp.where(wide < sizes_ref[0, b], density, 0.0)
        dens_ref[pl.ds(b, 1), :] = density
        for i in range(near):
            column = jnp.sum(parted[b, i] * density, axis=1, keepdims=True)
            gained = jnp.where(spot == i * batches + b, column, gained)
        return gained

    terms = lax.fori_loop(0, batches, batch, jnp.zeros((comps, 128), F32), unroll=True)
    top, low = pack(terms, pairs)
    packed[0:8] = top
    packed[8:16] = low

    early = list(started)
    for i in sorted(range(ny - 1), key=lambda i: -min(i + 1, ny - i - 1)):
        go(remote(packed, every.at[i + 1], ts.at[i], tr.at[i], ups[i]))
    every[0] = packed[...]
    for copy in early:
        copy.wait_send()
    turns = [0] + sorted(range(1, ny), key=lambda j: min(j, ny - j))
    for pair in range(ny // 2):
        lefts, rights = [], []
        for j in turns[2 * pair : 2 * pair + 2]:
            if j:
                remote(packed, every.at[j], ts.at[j - 1], tr.at[j - 1], up).wait_recv()
            value = unpack(every[j, 0:8], every[j, 8:16], pairs)
            high = value.astype(BF)
            rest = (value - high.astype(F32)).astype(BF)
            lefts.append(jnp.concatenate([high, rest], axis=0))
            rights.append(hot[(ny - j) % ny])
        gain = jnp.dot(
            jnp.concatenate(lefts, axis=1), jnp.concatenate(rights, axis=0), preferred_element_type=F32
        )
        if pair:
            gain = gain + sums[...]
        sums[...] = gain

    def answers_of(slot):
        lanes = slice(128 * slot, 128 * (slot + 1))
        return pack_sums(sums[0:32, lanes] + sums[32:64, lanes])

    far_first = sorted(range(1, NX * (1 + len(HOPS))), key=lambda n: -(min(n % NX, NX - n % NX) + (n >= NX)))
    for slot in far_first:
        h, dx = slot // NX, slot % NX
        answer[slot] = answers_of(slot)
        where = {"dev": y * NX + (x + dx) % NX}
        if h:
            where["region"] = (region - HOPS[h - 1] + regions) % regions
        go(remote(answer.at[slot], got.at[slot], zs.at[slot], zr.at[slot], where))
    gained = answers_of(0)
    for slot in reversed(far_first):
        remote(answer.at[slot], got.at[slot], zs.at[slot], zr.at[slot], right).wait_recv()
        gained = gained + got[slot]
    moment = unpack_sums(gained)
    upright = jnp.concatenate([moment, jnp.zeros((96, 128), F32)], axis=0).T
    mom_ref[...] = upright[pairs : pairs + ATOM_DEV, 0:comps]
    for b in range(batches):
        gathered = jnp.zeros((comps, points), F32)
        for i in range(near):
            q = i * batches + b
            gathered = gathered + radial[b, i] * moment[0:comps, q : q + 1]
        value = jnp.sum(gathered, axis=0, keepdims=True)
        pot_ref[b : b + 1, :] = jnp.where(wide < sizes_ref[0, b], value, 0.0)
    for copy in started[len(early) :]:
        copy.wait_send()


def hand_over(*arrays):
    def copies(*refs):
        for source, target in zip(refs[: len(arrays)], refs[len(arrays) :]):
            target[...] = source[...]

    vm = pl.BlockSpec(memory_space=pltpu.VMEM)
    return pl.pallas_call(
        copies,
        name="hand_over",
        out_shape=tuple(jax.ShapeDtypeStruct(a.shape, a.dtype) for a in arrays),
        in_specs=[vm] * len(arrays),
        out_specs=(vm,) * len(arrays),
    )(*arrays)


def per_device(
    basis_values,
    density_rows,
    block_mask,
    window_start,
    batch_offsets,
    batch_sizes,
    atom_near,
    harmonics,
    partition,
    radius,
    radial_table,
):
    devs = lax.axis_size("dev")
    ny = devs // NX
    slots, band, size, _ = density_rows.shape
    batches, near = atom_near.shape
    comps, knots = radial_table.shape
    points = basis_values.shape[2]
    dma = pltpu.SemaphoreType.DMA
    vm = pl.BlockSpec(memory_space=pltpu.VMEM)
    sm = pl.BlockSpec(memory_space=pltpu.SMEM)
    hb = pl.BlockSpec(memory_space=pl.ANY)
    block = (band, size, size)
    kept = (band, slots, size, size)
    hops = len(HOPS)
    density, moments, potential = pl.pallas_call(
        functools.partial(kernel, ny),
        name="whole_step",
        out_shape=(
            jax.ShapeDtypeStruct((batches, points), F32),
            jax.ShapeDtypeStruct((ATOM_DEV, comps), F32),
            jax.ShapeDtypeStruct((batches, points), F32),
        ),
        in_specs=[hb, sm, sm, sm, sm, vm, hb, hb, vm, hb, hb],
        out_specs=(vm, vm, vm),
        scratch_shapes=[
            pltpu.VMEM(density_rows.shape, BF),
            pltpu.VMEM(partition.shape, F32),
            pltpu.VMEM(radius.shape, F32),
            pltpu.VMEM(kept, BF),
            pltpu.VMEM((ny - 1,) + kept, BF),
            pltpu.VMEM((ny,) + block, BF),
            pltpu.VMEM((ny,) + block, BF),
            pltpu.VMEM((ny,) + block, BF),
            pltpu.VMEM((ny,) + block, BF),
            pltpu.VMEM((2, slots, size // 2, size), BF),
            pltpu.VMEM((ny, slots, size, size), BF),
            pltpu.VMEM((devs,) + block, BF),
            pltpu.VMEM((8, 128), jnp.int32),
            pltpu.VMEM((ny, NX, 4, 128), jnp.int32),
            pltpu.VMEM((hops, NX, 4, 128), jnp.int32),
            pltpu.VMEM(basis_values.shape, BF),
            pltpu.VMEM(harmonics.shape, BF),
            pltpu.VMEM((batches, band * size, points), BF),
            pltpu.VMEM((batches, near, comps, points), F32),
            pltpu.VMEM((batches, near, comps, points), F32),
            pltpu.VMEM((16, 128), F32),
            pltpu.VMEM((ny, 16, 128), F32),
            pltpu.VMEM((ny, 128, 128 * NX * (1 + hops)), BF),
            pltpu.VMEM((64, 128 * NX * (1 + hops)), F32),
            pltpu.VMEM((NX * (1 + hops), 24, 128), F32),
            pltpu.VMEM((NX * (1 + hops), 24, 128), F32),
            dma((ny - 1, CHUNKS)),
            dma((ny - 1, CHUNKS)),
            dma((ny + 3,)),
            dma((ny + 3,)),
            dma((hops,)),
            dma((hops,)),
            dma((ny, CHUNKS)),
            dma((ny, CHUNKS)),
            dma((ny, CHUNKS)),
            dma((ny, CHUNKS)),
            dma((ny, CHUNKS)),
            dma((ny, CHUNKS)),
            dma((ny, CHUNKS)),
            dma((ny, CHUNKS)),
            dma((4,)),
            dma((4,)),
            dma((ny - 1,)),
            dma((ny - 1,)),
            dma((ny - 1,)),
            dma((ny - 1,)),
            dma((NX * (1 + hops),)),
            dma((NX * (1 + hops),)),
            dma((5,)),
        ],
        compiler_params=pltpu.CompilerParams(collective_id=0, has_side_effects=True),
    )(
        density_rows,
        block_mask,
        window_start,
        batch_offsets,
        batch_sizes,
        atom_near.T,
        partition,
        radius,
        radial_table.T,
        basis_values,
        harmonics,
    )
    density, moments, potential = hand_over(density, moments, potential)
    return density, moments.T, potential


def solution(mesh):
    placed = (
        P(("region", "dev"), None, None, None),
        P(("region", "dev"), None, None, None),
        P(("region", "dev"), None),
        P(("region", "dev")),
        P(("region", "dev"), None),
        P(("region", "dev"), None),
        P(("region", "dev"), None),
        P(("region", "dev"), None, None, None),
        P(("region", "dev"), None, None),
        P(("region", "dev"), None, None),
        P(),
    )
    return jax.shard_map(
        per_device,
        mesh=mesh,
        in_specs=placed,
        out_specs=(
            P(("region", "dev"), None),
            P(None, ("region", "dev")),
            P(("region", "dev"), None),
        ),
        check_vma=False,
    )
```

```python
import functools

import jax
import jax.numpy as jnp
from jax import lax
from jax.experimental import pallas as pl
from jax.experimental.pallas import tpu as pltpu
from jax.sharding import PartitionSpec as P

ATOM_DEV = 16
NX = 4
CHUNKS = 2
HOPS = (1, 2, -1, -2)
MESH = pl.DeviceIdType.MESH
TN = (((0,), (0,)), ((), ()))
F32, BF = jnp.float32, jnp.bfloat16


def remote(src, dst, send_sem, recv_sem, where):
    return pltpu.make_async_remote_copy(
        src_ref=src,
        dst_ref=dst,
        send_sem=send_sem,
        recv_sem=recv_sem,
        device_id=where,
        device_id_type=MESH,
    )


def spline_values(radii, knots):
    knot = lax.broadcasted_iota(jnp.int32, (knots, radii.shape[1]), 0).astype(F32)
    distance = jnp.abs(radii - knot)
    inner = 2.0 / 3.0 - distance * distance + 0.5 * distance * distance * distance
    rest = 2.0 - distance
    outer = rest * rest * rest * (1.0 / 6.0)
    return jnp.where(distance < 1.0, inner, jnp.where(distance < 2.0, outer, 0.0))


def pack(terms, pairs):
    lane = lax.broadcasted_iota(jnp.int32, (8, 128), 1)
    row = lax.broadcasted_iota(jnp.int32, (8, 128), 0)
    third = terms[16:24]
    last = jnp.broadcast_to(terms[24:25], (8, 128))
    top = jnp.where(lane < pairs, terms[0:8], pltpu.roll(third, 72, 1))
    tail = jnp.where(row == 0, pltpu.roll(last, 88, 1), jnp.where(row == 1, pltpu.roll(last, 48, 1), 0.0))
    low = jnp.where(lane < pairs, terms[8:16], jnp.where(lane < 88, pltpu.roll(third, 16, 1), tail))
    return top, low


def unpack(top, low, pairs):
    lane = lax.broadcasted_iota(jnp.int32, (8, 128), 1)
    row = lax.broadcasted_iota(jnp.int32, (8, 128), 0)
    live = lane < pairs
    first = jnp.where(live, top, 0.0)
    second = jnp.where(live, low, 0.0)
    third = jnp.where(lane < 56, pltpu.roll(top, 56, 1), jnp.where(live, pltpu.roll(low, 112, 1), 0.0))
    zero = jnp.broadcast_to(low[0:1], (8, 128))
    one = jnp.broadcast_to(low[1:2], (8, 128))
    last = jnp.where(lane < 40, pltpu.roll(zero, 40, 1), jnp.where(live, pltpu.roll(one, 80, 1), 0.0))
    last = jnp.where(row == 0, last, 0.0)
    return jnp.concatenate([first, second, third, last], axis=0)


def pack_sums(sums):
    lane = lax.broadcasted_iota(jnp.int32, (8, 128), 1)
    row = lax.broadcasted_iota(jnp.int32, (8, 128), 0)
    last = jnp.broadcast_to(sums[24:25], (8, 128))
    tail = jnp.where(row == 1, pltpu.roll(last, 48, 1), jnp.where(row == 2, pltpu.roll(last, 8, 1), 0.0))
    tail = jnp.where(row == 0, pltpu.roll(last, 88, 1), tail)
    return jnp.concatenate([jnp.where(lane < 88, sums[0:8], tail), sums[8:24]], axis=0)


def unpack_sums(packed):
    lane = lax.broadcasted_iota(jnp.int32, (8, 128), 1)
    row = lax.broadcasted_iota(jnp.int32, (8, 128), 0)
    lines = [jnp.broadcast_to(packed[n : n + 1], (8, 128)) for n in range(3)]
    last = jnp.where(lane < 80, pltpu.roll(lines[1], 80, 1), pltpu.roll(lines[2], 120, 1))
    last = jnp.where(lane < 40, pltpu.roll(lines[0], 40, 1), last)
    return jnp.concatenate([packed, jnp.where((row == 0) & (lane < 88), last, 0.0)], axis=0)


def kernel(
    ny,
    rows_hbm,
    mask_ref,
    start_ref,
    offsets_ref,
    sizes_ref,
    near_ref,
    part_hbm,
    radius_hbm,
    radial_ref,
    basis_hbm,
    harm_hbm,
    dens_ref,
    mom_ref,
    pot_ref,
    rows_ref,
    part_ref,
    radius_ref,
    own,
    hold,
    out_r,
    out_l,
    out_o,
    relay,
    swap,
    across,
    win,
    line,
    metas,
    asked,
    basis,
    harm,
    turned,
    parted,
    radial,
    packed,
    every,
    hot,
    sums,
    answer,
    got,
    ys,
    yr,
    ms,
    mr,
    qs,
    qr,
    rs,
    ls,
    os_,
    fr,
    fl,
    fo,
    frel,
    fws,
    sws,
    swr,
    acs,
    acr,
    ts,
    tr,
    zs,
    zr,
    local,
):
    region, me = lax.axis_index("region"), lax.axis_index("dev")
    regions, devs = lax.axis_size("region"), ny * NX
    x, y = me % NX, me // NX
    far = ny // 2
    xr, xl, xo = (x + 1) % NX, (x + NX - 1) % NX, (x + 2) % NX
    right, left, other = ({"dev": y * NX + xx} for xx in (xr, xl, xo))
    ups = [{"dev": ((y + s) % ny) * NX + x} for s in range(1, ny)]
    up, down = ups[0], ups[-1]
    nears = [{"region": (region + h + regions) % regions} for h in HOPS]
    slots, band, size, _ = rows_ref.shape
    step = band // CHUNKS
    near, batches = near_ref.shape
    pairs = near * batches
    knots, comps = radial_ref.shape
    points = part_ref.shape[2]
    started = []

    def go(copy):
        copy.start()
        started.append(copy)

    barrier = pltpu.get_barrier_semaphore()
    greeted = [up, down, right, left, other] + nears
    for peer in greeted:
        pl.semaphore_signal(barrier, inc=1, device_id=peer, device_id_type=MESH)
    fetch_rows = pltpu.make_async_copy(rows_hbm, rows_ref, local.at[2])
    fetch_rows.start()
    fetches = [
        pltpu.make_async_copy(source, target, local.at[n])
        for source, target, n in (
            (basis_hbm, basis, 0),
            (harm_hbm, harm, 1),
            (part_hbm, part_ref, 3),
            (radius_hbm, radius_ref, 4),
        )
    ]

    lane = lax.broadcasted_iota(jnp.int32, (1, 128), 1)
    line[...] = jnp.zeros_like(line)
    line[0:near, 0:batches] = near_ref[...]
    total = jnp.zeros((1, 128), jnp.int32)
    for i in range(near):
        moved = pltpu.roll(jnp.broadcast_to(line[i : i + 1, :], (8, 128)), i * batches, 1)[0:1]
        total = jnp.where((lane >= i * batches) & (lane < (i + 1) * batches), moved, total)
    atom_region = ATOM_DEV * devs
    bits = atom_region.bit_length() - 1
    side = region + lax.shift_right_logical(total, bits) - 1
    side = jnp.where(side < 0, side + regions, jnp.where(side >= regions, side - regions, side))
    target = side * atom_region + (total & (atom_region - 1))
    owned = region * atom_region + me * ATOM_DEV + lane - pairs
    whole_line = jnp.where(lane < pairs, target, jnp.where(lane < pairs + ATOM_DEV, owned, -1))
    start = start_ref[0]
    line[0:1] = whole_line
    line[1:2] = jnp.full((1, 128), start // devs, jnp.int32)
    line[2:3] = jnp.full((1, 128), start % devs, jnp.int32)
    metas[0, x] = line[0:4]
    fetch_rows.wait()
    for t in range(slots):
        for k in range(band):
            keep = jnp.full((1, 1), mask_ref[t, k], jnp.int32).astype(F32).astype(BF)
            own[k, t] = rows_ref[t, k] * keep
    pl.semaphore_wait(barrier, len(greeted))

    def part_of(ref, c):
        return ref.at[pl.ds(c * step, step)]

    for c in range(CHUNKS):
        go(remote(part_of(own, c), part_of(hold.at[0], c), ys.at[0, c], yr.at[0, c], down))
        go(remote(part_of(own, c), part_of(hold.at[far], c), ys.at[far, c], yr.at[far, c], up))
        if c == 0:
            for i, peer in enumerate((right, left, other)):
                go(remote(line.at[0:4], metas.at[0, x], ms.at[i], mr.at[i], peer))

    for copy in fetches:
        copy.start()

    def row_meta(i):
        remote(line.at[0:4], metas.at[0, (xl, xr, xo)[i]], ms.at[i], mr.at[i], right).wait_recv()

    row_meta(0)
    row_meta(1)
    lone, halfway = band - 1, size // 2
    first_half, second_half = pl.ds(0, halfway), pl.ds(halfway, halfway)
    go(remote(own.at[lone, :, first_half], swap.at[0], sws.at[0], swr.at[0], right))
    go(remote(own.at[lone, :, second_half], swap.at[1], sws.at[1], swr.at[1], left))
    base = 3

    order = [0]
    for s in range(1, far + 1):
        order.append(s)
        if s < far:
            order.append(-s)

    def row_of(g):
        return (y + order[g] + ny) % ny

    def weights(xx, d):
        q = metas[0, xx, 1:2, :]
        m = metas[0, xx, 2:3, :]
        slot = q + jnp.where(m > d, 1, 0)
        slot = jnp.where(slot >= slots, slot - slots, slot)
        return [jnp.where(slot == t, 1.0, 0.0).astype(F32).astype(BF) for t in range(slots)]

    def other_part(c):
        low, high = c * step, min((c + 1) * step, lone)
        return pl.ds(low, high - low) if high > low else None

    def straight(g, c):
        return g == ny - 1 and c == CHUNKS - 1

    def via_right(g, c):
        return (g + c) % 2 == 0

    def process(g, c, some=(0, 1, 2, 3)):
        rho = order[g]
        d = row_of(g) * NX + x
        source = own if rho == 0 else hold.at[rho - 1 if rho > 0 else far - rho - 1]
        picks = ((xr, out_r.at[g]), (xl, out_l.at[g]), (xo, out_o.at[g]), (x, win.at[d]))
        picks = [(n, (picks[n][1], weights(picks[n][0], d))) for n in some]
        for k in range(c * step, (c + 1) * step):
            parts = [source[k, t] for t in range(slots)]
            for n, (dst, w) in picks:
                if n == 2 and k == lone:
                    continue
                chosen = parts[0] * w[0]
                for t in range(1, slots):
                    chosen = chosen + parts[t] * w[t]
                dst[k] = chosen
        if 2 in some and other_part(c) is not None:
            piece = other_part(c)
            if straight(g, c):
                go(remote(out_o.at[g, piece], win.at[d, piece], os_.at[g, c], fo.at[g, c], other))
            else:
                go(remote(out_o.at[g, piece], relay.at[g, piece], os_.at[g, c], frel.at[g, c], right if via_right(g, c) else left))
        if 0 not in some:
            return
        go(remote(part_of(out_r.at[g], c), part_of(win.at[d], c), rs.at[g, c], fl.at[g, c], right))
        go(remote(part_of(out_l.at[g], c), part_of(win.at[d], c), ls.at[g, c], fr.at[g, c], left))

    def passing(g, c):
        some = other_part(c)
        if some is None or straight(g, c):
            return
        toward, origin = (right, xl) if via_right(g, c) else (left, xr)
        d = row_of(g) * NX + origin
        remote(out_o.at[g, some], relay.at[g, some], os_.at[g, c], frel.at[g, c], right).wait_recv()
        go(remote(relay.at[g, some], win.at[d, some], fws.at[g, c], fo.at[g, c], toward))

    def take(g):
        rho = order[g]
        d = row_of(g) * NX + xo
        source = across.at[0 if rho == 0 else (rho if rho > 0 else far - rho)]
        w = weights(x, d)
        chosen = source[0] * w[0]
        for t in range(1, slots):
            chosen = chosen + source[t] * w[t]
        win[d, lone] = chosen

    def across_in(s):
        i, j = s - 1, far + s - 1
        remote(across.at[0], across.at[1 + i], acs.at[i], acr.at[i], down).wait_recv()
        if s < far:
            go(remote(across.at[1 + i], across.at[2 + i], acs.at[i + 1], acr.at[i + 1], down))
            remote(across.at[0], across.at[1 + j], acs.at[j], acr.at[j], up).wait_recv()
            if s < far - 1:
                go(remote(across.at[1 + j], across.at[2 + j], acs.at[j + 1], acr.at[j + 1], up))
        take(2 * s - 1)
        if s < far:
            take(2 * s)

    def prepare(b, carry):
        for j in range(band):
            turned[b, j * size : (j + 1) * size, :] = basis[b, j].T
        for i in range(near):
            values = harm[b, i].astype(F32)
            parted[b, i] = values * part_ref[b, i : i + 1, :]
            spline = spline_values(radius_ref[b, i : i + 1, :], knots)
            curve = lax.dot_general(
                radial_ref[...], spline, TN, precision=lax.Precision.HIGHEST, preferred_element_type=F32
            )
            radial[b, i] = values * curve
        return carry

    def fill(some):
        def one(rho, carry):
            column = jnp.broadcast_to(metas[rho, x, 0:1, :], (128, 128)).T
            for h in some:
                for dx in range(NX):
                    xx = (x + dx) % NX
                    line_of = metas[0, xx, 0:1, :] if h == 0 else asked[h - 1, xx, 0:1, :]
                    same = jnp.where(column == line_of, 1.0, 0.0).astype(F32)
                    slot = h * NX + dx
                    hot[rho, :, 128 * slot : 128 * (slot + 1)] = same.astype(BF)
            return carry

        lax.fori_loop(0, ny, one, 0)

    for c in range(CHUNKS):
        process(0, c, (0, 1))
    row_meta(2)
    for i in range(len(HOPS)):
        go(remote(metas.at[0], asked.at[i], qs.at[i], qr.at[i], nears[i]))
    go(remote(metas.at[0], metas.at[1], ms.at[base], mr.at[base], down))
    go(remote(metas.at[0], metas.at[ny - 1], ms.at[base + far], mr.at[base + far], up))
    for c in range(CHUNKS):
        process(0, c, (2, 3))
    remote(own.at[lone, :, first_half], swap.at[0], sws.at[0], swr.at[0], right).wait_recv()
    go(remote(swap.at[0], across.at[0, :, first_half], sws.at[2], swr.at[2], right))
    remote(own.at[lone, :, second_half], swap.at[1], sws.at[1], swr.at[1], left).wait_recv()
    go(remote(swap.at[1], across.at[0, :, second_half], sws.at[3], swr.at[3], left))
    for copy in fetches:
        copy.wait()
    per = -(-batches // (CHUNKS * (far - 1)))
    ready = 0
    lag = []
    for s in range(1, far + 1):
        i, j = s - 1, far + s - 1
        for c in range(CHUNKS):
            remote(part_of(own, c), part_of(hold.at[i], c), ys.at[i, c], yr.at[i, c], down).wait_recv()
            if s < far - 1 or (s < far and c % 2 == 0):
                go(remote(part_of(hold.at[i], c), part_of(hold.at[i + 1], c), ys.at[i + 1, c], yr.at[i + 1, c], down))
            if s < far:
                remote(part_of(own, c), part_of(hold.at[j], c), ys.at[j, c], yr.at[j, c], up).wait_recv()
                if s < far - 1:
                    go(remote(part_of(hold.at[j], c), part_of(hold.at[j + 1], c), ys.at[j + 1, c], yr.at[j + 1, c], up))
                elif c % 2 == 1:
                    go(remote(part_of(hold.at[j], c), part_of(hold.at[far - 1], c), ys.at[far - 1, c], yr.at[far - 1, c], up))
            if c == 0:
                remote(metas.at[0], metas.at[s], ms.at[base + i], mr.at[base + i], down).wait_recv()
                if s < far:
                    go(remote(metas.at[s], metas.at[s + 1], ms.at[base + i + 1], mr.at[base + i + 1], down))
                    remote(metas.at[0], metas.at[ny - s], ms.at[base + j], mr.at[base + j], up).wait_recv()
                    if s < far - 1:
                        go(remote(metas.at[ny - s], metas.at[ny - s - 1], ms.at[base + j + 1], mr.at[base + j + 1], up))
            process(2 * s - 1, c)
            if s < far:
                process(2 * s, c)
            if s == 1:
                lag.append((0, c))
            else:
                lag.append((2 * s - 3, c))
                lag.append((2 * s - 2, c))
            while lag:
                passing(*lag.pop(0))
            if ready < batches and s < far:
                upto = min(batches, ready + per)
                lax.fori_loop(ready, upto, prepare, 0)
                ready = upto
        if s == 1:
            remote(swap.at[0], across.at[0, :, first_half], sws.at[2], swr.at[2], right).wait_recv()
            remote(swap.at[1], across.at[0, :, second_half], sws.at[3], swr.at[3], left).wait_recv()
            go(remote(across.at[0], across.at[1], acs.at[0], acr.at[0], down))
            go(remote(across.at[0], across.at[1 + far], acs.at[far], acr.at[far], up))
            take(0)
        else:
            across_in(s - 1)
    for i in range(len(HOPS)):
        remote(metas.at[0], asked.at[i], qs.at[i], qr.at[i], nears[0]).wait_recv()
    fill((0, 1))
    for c in range(CHUNKS):
        passing(ny - 1, c)
    fill(tuple(range(2, 1 + len(HOPS))))
    across_in(far)
    for g in range(ny):
        row = row_of(g) * NX
        for c in range(CHUNKS):
            remote(part_of(out_r.at[g], c), part_of(win.at[row + xl], c), rs.at[g, c], fl.at[g, c], right).wait_recv()
            remote(part_of(out_l.at[g], c), part_of(win.at[row + xr], c), ls.at[g, c], fr.at[g, c], left).wait_recv()
            some = other_part(c)
            if some is not None:
                remote(out_o.at[g, some], win.at[row + xo, some], fws.at[g, c], fo.at[g, c], right).wait_recv()

    zero = jnp.zeros((size, size), BF)
    wide = lax.broadcasted_iota(jnp.int32, (1, points), 1)
    spot = lax.broadcasted_iota(jnp.int32, (comps, 128), 1)

    def batch(b, gained):
        first = start + offsets_ref[0, b]
        places = [lax.rem(first + j, devs) for j in range(band)]

        def piece(j, k):
            return win[places[j], k]

        def quad(a, b_, c, d):
            return jnp.concatenate([jnp.concatenate([a, b_], axis=1), jnp.concatenate([c, d], axis=1)], axis=0)

        low, high = turned[b, 0 : 2 * size, :], turned[b, 2 * size : 4 * size, :]
        dot = functools.partial(jnp.dot, preferred_element_type=F32)
        m01 = dot(quad(piece(0, 1), piece(0, 2), piece(1, 0), piece(1, 1)), low)
        m01 = m01 + dot(quad(piece(0, 3), zero, piece(1, 2), piece(1, 3)), high)
        m23 = dot(quad(piece(2, 1), piece(2, 2), piece(3, 0), piece(3, 1)), high)
        m2x = dot(piece(2, 0), turned[b, size : 2 * size, :])
        density = jnp.sum(m01 * low.astype(F32) + m23 * high.astype(F32), axis=0, keepdims=True)
        density = density + jnp.sum(m2x * turned[b, 2 * size : 3 * size, :].astype(F32), axis=0, keepdims=True)
        density = jnp.where(wide < sizes_ref[0, b], density, 0.0)
        dens_ref[pl.ds(b, 1), :] = density
        for i in range(near):
            column = jnp.sum(parted[b, i] * density, axis=1, keepdims=True)
            gained = jnp.where(spot == i * batches + b, column, gained)
        return gained

    terms = lax.fori_loop(0, batches, batch, jnp.zeros((comps, 128), F32), unroll=True)
    top, low = pack(terms, pairs)
    packed[0:8] = top
    packed[8:16] = low

    early = list(started)
    for i in sorted(range(ny - 1), key=lambda i: -min(i + 1, ny - i - 1)):
        go(remote(packed, every.at[i + 1], ts.at[i], tr.at[i], ups[i]))
    every[0] = packed[...]
    for copy in early:
        copy.wait_send()
    turns = [0] + sorted(range(1, ny), key=lambda j: min(j, ny - j))
    for pair in range(ny // 2):
        lefts, rights = [], []
        for j in turns[2 * pair : 2 * pair + 2]:
            if j:
                remote(packed, every.at[j], ts.at[j - 1], tr.at[j - 1], up).wait_recv()
            value = unpack(every[j, 0:8], every[j, 8:16], pairs)
            high = value.astype(BF)
            rest = (value - high.astype(F32)).astype(BF)
            lefts.append(jnp.concatenate([high, rest], axis=0))
            rights.append(hot[(ny - j) % ny])
        gain = jnp.dot(
            jnp.concatenate(lefts, axis=1), jnp.concatenate(rights, axis=0), preferred_element_type=F32
        )
        if pair:
            gain = gain + sums[...]
        sums[...] = gain

    def answers_of(slot):
        lanes = slice(128 * slot, 128 * (slot + 1))
        return pack_sums(sums[0:32, lanes] + sums[32:64, lanes])

    far_first = sorted(range(1, NX * (1 + len(HOPS))), key=lambda n: -(min(n % NX, NX - n % NX) + (n >= NX)))
    for slot in far_first:
        h, dx = slot // NX, slot % NX
        answer[slot] = answers_of(slot)
        where = {"dev": y * NX + (x + dx) % NX}
        if h:
            where["region"] = (region - HOPS[h - 1] + regions) % regions
        go(remote(answer.at[slot], got.at[slot], zs.at[slot], zr.at[slot], where))
    gained = answers_of(0)
    for slot in reversed(far_first):
        remote(answer.at[slot], got.at[slot], zs.at[slot], zr.at[slot], right).wait_recv()
        gained = gained + got[slot]
    moment = unpack_sums(gained)
    upright = jnp.concatenate([moment, jnp.zeros((96, 128), F32)], axis=0).T
    mom_ref[...] = upright[pairs : pairs + ATOM_DEV, 0:comps]
    for b in range(batches):
        gathered = jnp.zeros((comps, points), F32)
        for i in range(near):
            q = i * batches + b
            gathered = gathered + radial[b, i] * moment[0:comps, q : q + 1]
        value = jnp.sum(gathered, axis=0, keepdims=True)
        pot_ref[b : b + 1, :] = jnp.where(wide < sizes_ref[0, b], value, 0.0)
    for copy in started[len(early) :]:
        copy.wait_send()


def hand_over(*arrays):
    count = len(arrays)

    def copies(*refs):
        sems = refs[2 * count]
        moves = [pltpu.make_async_copy(refs[n], refs[count + n], sems.at[n]) for n in range(count)]
        for move in moves:
            move.start()
        for move in moves:
            move.wait()

    hb = pl.BlockSpec(memory_space=pl.ANY)
    return pl.pallas_call(
        copies,
        name="hand_over",
        out_shape=tuple(jax.ShapeDtypeStruct(a.shape, a.dtype) for a in arrays),
        in_specs=[hb] * count,
        out_specs=(hb,) * count,
        scratch_shapes=[pltpu.SemaphoreType.DMA((count,))],
    )(*arrays)


def per_device(
    basis_values,
    density_rows,
    block_mask,
    window_start,
    batch_offsets,
    batch_sizes,
    atom_near,
    harmonics,
    partition,
    radius,
    radial_table,
):
    devs = lax.axis_size("dev")
    ny = devs // NX
    slots, band, size, _ = density_rows.shape
    batches, near = atom_near.shape
    comps, knots = radial_table.shape
    points = basis_values.shape[2]
    dma = pltpu.SemaphoreType.DMA
    vm = pl.BlockSpec(memory_space=pltpu.VMEM)
    sm = pl.BlockSpec(memory_space=pltpu.SMEM)
    hb = pl.BlockSpec(memory_space=pl.ANY)
    block = (band, size, size)
    kept = (band, slots, size, size)
    hops = len(HOPS)
    density, moments, potential = pl.pallas_call(
        functools.partial(kernel, ny),
        name="whole_step",
        out_shape=(
            jax.ShapeDtypeStruct((batches, points), F32),
            jax.ShapeDtypeStruct((ATOM_DEV, comps), F32),
            jax.ShapeDtypeStruct((batches, points), F32),
        ),
        in_specs=[hb, sm, sm, sm, sm, vm, hb, hb, vm, hb, hb],
        out_specs=(vm, vm, vm),
        scratch_shapes=[
            pltpu.VMEM(density_rows.shape, BF),
            pltpu.VMEM(partition.shape, F32),
            pltpu.VMEM(radius.shape, F32),
            pltpu.VMEM(kept, BF),
            pltpu.VMEM((ny - 1,) + kept, BF),
            pltpu.VMEM((ny,) + block, BF),
            pltpu.VMEM((ny,) + block, BF),
            pltpu.VMEM((ny,) + block, BF),
            pltpu.VMEM((ny,) + block, BF),
            pltpu.VMEM((2, slots, size // 2, size), BF),
            pltpu.VMEM((ny, slots, size, size), BF),
            pltpu.VMEM((devs,) + block, BF),
            pltpu.VMEM((8, 128), jnp.int32),
            pltpu.VMEM((ny, NX, 4, 128), jnp.int32),
            pltpu.VMEM((hops, NX, 4, 128), jnp.int32),
            pltpu.VMEM(basis_values.shape, BF),
            pltpu.VMEM(harmonics.shape, BF),
            pltpu.VMEM((batches, band * size, points), BF),
            pltpu.VMEM((batches, near, comps, points), F32),
            pltpu.VMEM((batches, near, comps, points), F32),
            pltpu.VMEM((16, 128), F32),
            pltpu.VMEM((ny, 16, 128), F32),
            pltpu.VMEM((ny, 128, 128 * NX * (1 + hops)), BF),
            pltpu.VMEM((64, 128 * NX * (1 + hops)), F32),
            pltpu.VMEM((NX * (1 + hops), 24, 128), F32),
            pltpu.VMEM((NX * (1 + hops), 24, 128), F32),
            dma((ny - 1, CHUNKS)),
            dma((ny - 1, CHUNKS)),
            dma((ny + 3,)),
            dma((ny + 3,)),
            dma((hops,)),
            dma((hops,)),
            dma((ny, CHUNKS)),
            dma((ny, CHUNKS)),
            dma((ny, CHUNKS)),
            dma((ny, CHUNKS)),
            dma((ny, CHUNKS)),
            dma((ny, CHUNKS)),
            dma((ny, CHUNKS)),
            dma((ny, CHUNKS)),
            dma((4,)),
            dma((4,)),
            dma((ny - 1,)),
            dma((ny - 1,)),
            dma((ny - 1,)),
            dma((ny - 1,)),
            dma((NX * (1 + hops),)),
            dma((NX * (1 + hops),)),
            dma((5,)),
        ],
        compiler_params=pltpu.CompilerParams(collective_id=0, has_side_effects=True),
    )(
        density_rows,
        block_mask,
        window_start,
        batch_offsets,
        batch_sizes,
        atom_near.T,
        partition,
        radius,
        radial_table.T,
        basis_values,
        harmonics,
    )
    density, moments, potential = hand_over(density, moments, potential)
    return density, moments.T, potential


def solution(mesh):
    placed = (
        P(("region", "dev"), None, None, None),
        P(("region", "dev"), None, None, None),
        P(("region", "dev"), None),
        P(("region", "dev")),
        P(("region", "dev"), None),
        P(("region", "dev"), None),
        P(("region", "dev"), None),
        P(("region", "dev"), None, None, None),
        P(("region", "dev"), None, None),
        P(("region", "dev"), None, None),
        P(),
    )
    return jax.shard_map(
        per_device,
        mesh=mesh,
        in_specs=placed,
        out_specs=(
            P(("region", "dev"), None),
            P(None, ("region", "dev")),
            P(("region", "dev"), None),
        ),
        check_vma=False,
    )
```
